128 devices in a mesh: row: 16 (over x, y), col: 8 (over z, core).
Axes of the slice: x: 4, y: 4, z: 4, core: 2. Of those that a mesh axis runs over, the one named last changes fastest.
Arguments:
- rhs_rows: float32 [65536, 256], P(('row', 'col')), may hold values from -6 to 6
- dest_row: int32 [65536], P(('row', 'col')), may hold values from 0 to 65535, as said below
- diag_inverse: bfloat16 [4, 128, 128, 128], P(None, ('row', 'col')), may hold values from -1 to 1.5, as said below
- lower_blocks: bfloat16 [3, 16, 8, 128, 8, 16, 128], P(None, 'row', None, None, 'col'), may hold values from -0.046875 to 0.046875
- block_mask: int32 [3, 16, 8, 8, 16], P(None, 'row', None, 'col'), may hold values 0 or 1
Outputs:
- solution: bfloat16 [4, 128, 128, 256], P(None, ('row', 'col'))
The draws below stay inside these ranges and needn't reach their ends.
Inputs may be any that keep to these rules, and one draw needn't show every extreme that they name: dest_row is a permutation of the rows. In each aligned block of 512 entries, exactly 4 entries g have (g // 128) % 128 equal to q, for every supernode index q. `diag_inverse`: every block is lower triangular with positive diagonal entries.
All inputs are finite; a program needn't handle non-finite values. No bound on the sum of `block_mask` on one device may be relied on, other than what follows from the above.
Results may differ from the reference program's by a relative error of at most 0.029.
Values may be sent and summed in bfloat16 or wider, within the bound.
A program may use at most 128 MiB of HBM per device.

```python
import math
import jax
import jax.numpy as jnp
from jax import lax

B = 128
NRHS = 256
NLEV = 4
OWNERS = 16
HOLDERS = 8
S = 128
LEVM = 3
NROWS = 65536
GROUP = 4


def draw_dest_row(key, part):
    rows_dev = NLEV * B
    key_owner, key_source = jax.random.split(key)
    owner_keys = jax.random.split(key_owner, S)
    local_perm = jax.vmap(lambda sub_key: jax.random.permutation(sub_key, rows_dev))(owner_keys)
    by_source = local_perm.reshape(S, S, GROUP).transpose(1, 0, 2)
    level_idx = by_source // B
    within = by_source % B
    owner_idx = jnp.arange(S, dtype=jnp.int32)[None, :, None]
    global_row = (level_idx * S + owner_idx) * B + within
    flat_rows = global_row.reshape(S, rows_dev)
    source_keys = jax.random.split(key_source, S)
    shuffle = jax.vmap(lambda sub_key: jax.random.permutation(sub_key, rows_dev))(source_keys)
    placed = jnp.take_along_axis(flat_rows, shuffle, axis=1)
    return placed.reshape(NROWS).astype(jnp.int32)


def draw_diag_inverse(key, part):
    key_noise, key_diag = jax.random.split(key)
    shape = (NLEV, S, B, B)
    row_idx = lax.broadcasted_iota(jnp.int32, shape, 2)
    col_idx = lax.broadcasted_iota(jnp.int32, shape, 3)
    noise = jax.random.normal(key_noise, shape, jnp.float32) * (0.5 / math.sqrt(B))
    diagonal = jax.random.uniform(key_diag, shape, jnp.float32, 0.6, 1.4)
    values = jnp.where(row_idx > col_idx, noise, jnp.where(row_idx == col_idx, diagonal, 0.0))
    return values.astype(jnp.bfloat16)


def with_ends(values, stream_key, least, high):
    place = [jax.random.randint(jax.random.fold_in(stream_key, axis), (), 0, length) for axis, length in enumerate(values.shape)]
    widest = values.shape.index(max(values.shape))
    neighbour = place[:widest] + [(place[widest] + 1) % values.shape[widest]] + place[widest + 1:]
    return values.at[tuple(place)].set(least).at[tuple(neighbour)].set(high)


def levels(key, extent, pieces, smallest, high):
    def one(axis_at, blocks):
        heights = jax.random.uniform(jax.random.fold_in(jax.random.fold_in(key, 6), axis_at), (blocks,), jnp.float32, smallest / len(pieces), high / len(pieces))
        return jnp.repeat(jnp.exp(heights), extent[axis_at] // blocks).reshape((-1,) + (1,) * (len(extent) - axis_at - 1))

    factor_of = one(*pieces[0])
    for cut in pieces[1:]:
        factor_of = factor_of * one(*cut)
    return factor_of


def centred(key, shape, scale, reach, cuts=(), kind=jnp.bfloat16):
    entries = scale * jax.random.normal(key, shape, jnp.float32)
    if cuts:
        entries = entries * levels(key, shape, cuts, -0.22, 0.18)
    return jnp.clip(entries, -reach, reach).astype(kind)


def setup_inputs(seed: int = 0) -> dict:
    keys = jax.random.split(jax.random.key(seed), 6)
    rhs_rows = centred(keys[0], (NROWS, NRHS), 1.0, 6.0, ((0, 128),), jnp.float32)
    dest_row = draw_dest_row(jax.random.fold_in(keys[5], 71), 0)
    diag_inverse = draw_diag_inverse(jax.random.fold_in(keys[5], 71), 0)
    lower_blocks = centred(keys[3], (LEVM, OWNERS, HOLDERS, B, HOLDERS, OWNERS, B), (S * B) ** -0.5, 0.046875, ((1, 16), (4, 8)))
    block_mask = with_ends((jax.random.randint(keys[4], (LEVM, OWNERS, HOLDERS, HOLDERS, OWNERS), 0, 2) < 1).astype(jnp.int32), jax.random.fold_in(keys[4], 1), 0, 1)
    return {"rhs_rows": rhs_rows, "dest_row": dest_row, "diag_inverse": diag_inverse, "lower_blocks": lower_blocks, "block_mask": block_mask}


def couple_down(blocks, mask_level, earlier):
    earlier_f = earlier.reshape(OWNERS, HOLDERS, B, NRHS).astype(jnp.float32)

    def one_owner(inputs):
        row_blocks, row_mask = inputs
        weights = row_blocks.astype(jnp.float32) * row_mask[:, None, :, :, None].astype(jnp.float32)
        partials = jnp.einsum('ikcpj,pcjn->ickn', weights, earlier_f)
        partials = lax.optimization_barrier(partials.astype(jnp.bfloat16)).astype(jnp.float32)
        return jnp.sum(partials, axis=1)

    return lax.map(one_owner, (blocks, mask_level)).reshape(S, B, NRHS)


def couple_up(blocks, mask_level, upper):
    upper_f = upper.reshape(OWNERS, HOLDERS, B, NRHS).astype(jnp.float32)

    def one_owner(carry, inputs):
        row_blocks, row_mask, row_upper = inputs
        weights = row_blocks.astype(jnp.float32) * row_mask[:, None, :, :, None].astype(jnp.float32)
        partial_value = jnp.einsum('ikcpj,ikn->pcjn', weights, row_upper)
        partial_value = lax.optimization_barrier(partial_value.astype(jnp.bfloat16)).astype(jnp.float32)
        return carry + partial_value, None

    start_sum = jnp.zeros((OWNERS, HOLDERS, B, NRHS), jnp.float32)
    totals = lax.scan(one_owner, start_sum, (blocks, mask_level, upper_f))[0]
    return totals.reshape(S, B, NRHS)


def reference(rhs_rows, dest_row, diag_inverse, lower_blocks, block_mask):
    ordered = jnp.zeros_like(rhs_rows).at[dest_row].set(rhs_rows).reshape(NLEV, S, B, NRHS)
    solved = []
    for level_idx in range(NLEV):
        if level_idx == 0:
            residual = ordered[0].astype(jnp.bfloat16)
        else:
            coupled = couple_down(lower_blocks[level_idx - 1], block_mask[level_idx - 1], solved[level_idx - 1])
            residual = (ordered[level_idx] - coupled).astype(jnp.bfloat16)
        product = jnp.einsum('qab,qbn->qan', diag_inverse[level_idx].astype(jnp.float32), residual.astype(jnp.float32))
        solved.append(product.astype(jnp.bfloat16))
    solution = [None] * NLEV
    for level_idx in range(NLEV - 1, -1, -1):
        if level_idx == NLEV - 1:
            residual = solved[level_idx]
        else:
            back_coupled = couple_up(lower_blocks[level_idx], block_mask[level_idx], solution[level_idx + 1])
            residual = (solved[level_idx].astype(jnp.float32) - back_coupled).astype(jnp.bfloat16)
        product = jnp.einsum('qba,qbn->qan', diag_inverse[level_idx].astype(jnp.float32), residual.astype(jnp.float32))
        solution[level_idx] = product.astype(jnp.bfloat16)
    return jnp.stack(solution)
```

```python
import functools

import jax
import jax.numpy as jnp
from jax import lax
from jax.experimental import pallas as pl
from jax.experimental.pallas import tpu as pltpu
from jax.sharding import PartitionSpec as P

B = 128
NLEV = 4
N = 256
MESH = pl.DeviceIdType.MESH
F32 = jnp.float32
BF16 = jnp.bfloat16


def dot(a, b):
    return jnp.dot(a, b, preferred_element_type=F32)


def solve_kernel(
    ordered_ref, diag_ref, mask_ref, w_hbm, out_ref,
    raw, wd, gath, acc, sib_out, sib_in, z_out, z_in, solved_t, upper, part_out, part_in, line_out, line_in,
    load_sem, ag_s, ag_r, sib_s, sib_r, z_s, z_r, up_s, up_r, fw_s, fw_r, p1_s, p1_r, p2_s, p2_r,
):
    row = lax.axis_index("row")
    col = lax.axis_index("col")
    x, y = row // 4, row % 4
    z, core = col // 2, col % 2
    other = 1 - core

    def row_of(h, u, v):
        return (u % 4) * 4 + v % 4 if h == 0 else (v % 4) * 4 + u % 4

    first = (x, y)
    second = (y, x)

    def remote(src, dst, ssem, rsem, dev):
        return pltpu.make_async_remote_copy(
            src_ref=src, dst_ref=dst, send_sem=ssem, recv_sem=rsem, device_id=dev, device_id_type=MESH
        )

    sibling = (row, z * 2 + other)

    def z_peer(d):
        return (row, ((z + d) % 4) * 2 + core)

    barrier = pltpu.get_barrier_semaphore()
    peers = [sibling] + [z_peer(d) for d in (1, 2, 3)]
    peers += [(row_of(0, x + d, y), col) for d in (1, 2, 3)]
    peers += [(row_of(0, x, y + d), col) for d in (1, 2, 3)]
    for dev in peers:
        pl.semaphore_signal(barrier, inc=1, device_id=dev, device_id_type=MESH)

    loads = [pltpu.make_async_copy(w_hbm.at[l, 0, :, :, 0], raw.at[l], load_sem.at[l]) for l in range(3)]
    for load in loads:
        load.start()

    out_row = lax.broadcasted_iota(jnp.int32, (256, 256), 0)
    in_row = lax.broadcasted_iota(jnp.int32, (256, 256), 1)
    perm = jnp.where(in_row == (out_row % 16) * 16 + out_row // 16, 1.0, 0.0).astype(BF16)

    def relayout(l):
        def one(i, carry):
            zz, cc = i // 2, i % 2
            scale = [mask_ref[l, i * 16 + p].astype(F32) for p in range(16)]
            for k0 in range(0, 8, 2):
                piece = jnp.concatenate(
                    [raw[l, i, (k0 + s) * 16:(k0 + s + 1) * 16].reshape(256, B) for s in range(2)], axis=1
                )
                moved = dot(perm, piece)
                for p in range(16):
                    for s in range(2):
                        tile = moved[p * 16:(p + 1) * 16, s * B:(s + 1) * B] * scale[p]
                        wd[l, p, cc, zz, (k0 + s) * 16:(k0 + s + 1) * 16, :] = tile.astype(BF16)
            return carry

        lax.fori_loop(0, 8, one, 0)

    def put_solved(l, residual):
        solved = dot(diag_ref[l], residual).astype(BF16)
        return solved

    level0 = put_solved(0, ordered_ref[0].astype(BF16))
    gath[0, 0, row] = level0[:, :B]
    gath[0, 1, row] = level0[:, B:]
    solved_t[0] = level0.astype(F32).T
    pl.semaphore_wait(barrier, len(peers))

    def gather_copy(l, h, slot, idx, dev):
        return remote(gath.at[l, h, slot], gath.at[l, h, slot], ag_s.at[l, h, idx], ag_r.at[l, h, idx], dev)

    def pair_rhs(l, p):
        return jnp.concatenate([gath[l, 0, p], gath[l, 1, p]], axis=1)

    def down(l, carry):
        for h in range(2):
            u, v = first if h == 0 else second
            for d in (2, 1, 3):
                gather_copy(l, h, row, d - 1, (row_of(h, u + d, v), col)).start()
        for e in (0, 1, 3, 2):
            for h in range(2):
                u, v = first if h == 0 else second
                slot = row_of(h, u - e, v)
                if e:
                    gather_copy(l, h, slot, e - 1, (row, col)).wait_recv()
                for d in (2, 1, 3):
                    gather_copy(l, h, slot, 3 + e * 3 + d - 1, (row_of(h, u, v + d), col)).start()
            if e == 0:
                loads_wait(l)
                relayout(l)
        order = [(a, b) for a in (0, 1, 3) for b in (0, 1, 3)] + [(a, b) for a in range(4) for b in range(4) if 2 in (a, b)]
        done = set()

        def arrive(a, b):
            for h in range(2):
                e, d = (a, b) if h == 0 else (b, a)
                u, v = first if h == 0 else second
                if d and (h, e, d) not in done:
                    done.add((h, e, d))
                    gather_copy(l, h, row_of(h, u - e, v - d), 3 + e * 3 + d - 1, (row, col)).wait_recv()

        def operands(some):
            slots = [row_of(0, x - a, y - b) for a, b in some]
            rhs = jnp.concatenate([pair_rhs(l, p) for p in slots], axis=0)
            return slots, rhs

        def lhs(slots, c, r, n):
            return jnp.concatenate([wd[l, p, c, r:r + n].reshape(n * B, B) for p in slots], axis=1)

        for a, b in order[:8]:
            arrive(a, b)
        slots, rhs = operands(order[:8])
        for c in range(2):
            for r in range(0, 4, 2):
                acc[c, r:r + 2] = dot(lhs(slots, c, r, 2), rhs).reshape(2, B, N)
        for a, b in order[8:]:
            arrive(a, b)
        slots, rhs = operands(order[8:])
        for step, c in enumerate((other, core)):
            for half in range(2):
                r = ((z // 2 + 1 - half) % 2) * 2
                left = jnp.concatenate([wd[l, p, c, pl.ds(r, 2)].reshape(2 * B, B) for p in slots], axis=1)
                total = acc[c, pl.ds(r, 2)] + dot(left, rhs).reshape(2, B, N)
                if step == 0:
                    sib_out[l, pl.ds(r, 2)] = total.astype(BF16)
                    for s in range(2):
                        remote(sib_out.at[l, r + s], sib_in.at[l, r + s], sib_s.at[l, half * 2 + s], sib_r.at[l, r + s], sibling).start()
                else:
                    acc[c, pl.ds(r, 2)] = total
        for d in (2, 1, 3, 0):
            zz = (z + d) % 4
            remote(sib_out.at[l, zz], sib_in.at[l, zz], sib_s.at[l, 0], sib_r.at[l, zz], sibling).wait_recv()
            total = acc[core, zz] + sib_in[l, zz].astype(F32)
            if d:
                z_out[l, d - 1] = total.astype(BF16)
                remote(z_out.at[l, d - 1], z_in.at[l, d - 1], z_s.at[l, d - 1], z_r.at[l, d - 1], z_peer(d)).start()
            else:
                own = total
        for d in (1, 3, 2):
            remote(z_out.at[l, d - 1], z_in.at[l, d - 1], z_s.at[l, d - 1], z_r.at[l, d - 1], z_peer(d)).wait_recv()
            own = own + z_in[l, d - 1].astype(F32)
        residual = (ordered_ref[l + 1] - own).astype(BF16)
        solved = put_solved(l + 1, residual)
        gath[l + 1, 0, row] = solved[:, :B]
        gath[l + 1, 1, row] = solved[:, B:]
        solved_t[l + 1] = solved.astype(F32).T
        return carry

    def loads_wait(l):
        pltpu.make_async_copy(w_hbm.at[l, 0, :, :, 0], raw.at[l], load_sem.at[l]).wait()

    lax.fori_loop(0, 3, down, 0)

    def finish(l, slot, residual_t):
        sol_t = dot(residual_t.astype(BF16), diag_ref[l]).astype(BF16)
        upper[slot, core, z] = sol_t
        return sol_t

    top = finish(3, 0, solved_t[3])
    out_ref[3] = top.astype(F32).T.astype(BF16)

    def up_copy(t, d):
        return remote(upper.at[t, core, z], upper.at[t, core, z], up_s.at[t, d - 1], up_r.at[t, d - 1], z_peer(d))

    def forward_copy(t, d):
        slot = upper.at[t, core, (z - d) % 4]
        return remote(slot, slot, fw_s.at[t, d], fw_r.at[t, d], sibling)

    def part_copy(t, h, du, dv):
        u, v = first if h == 0 else second
        return remote(
            part_out.at[t, h, du, dv], part_in.at[t, h, du, dv],
            p1_s.at[t, h, du, dv], p1_r.at[t, h, du, dv], (row_of(h, u + du, v), col),
        )

    def line_copy(t, h, dv):
        u, v = first if h == 0 else second
        return remote(
            line_out.at[t, h, dv], line_in.at[t, h, dv], p2_s.at[t, h, dv], p2_r.at[t, h, dv], (row_of(h, u, v + dv), col)
        )

    def up(t, carry):
        l = 2 - t
        for d in (2, 1, 3):
            up_copy(t, d).start()
        forward_copy(t, 0).start()
        for d in (1, 3, 2):
            slot = upper.at[t, core, (z - d) % 4]
            remote(slot, slot, up_s.at[t, d - 1], up_r.at[t, d - 1], sibling).wait_recv()
            forward_copy(t, d).start()
        for d in (0, 1, 3, 2):
            slot = upper.at[t, other, (z - d) % 4]
            remote(slot, slot, fw_s.at[t, d], fw_r.at[t, d], sibling).wait_recv()
        left = jnp.concatenate([upper[t, c, r] for c in range(2) for r in range(4)], axis=1)
        pairs = [((2, 2), (2, 1)), ((2, 3), (2, 0)), ((1, 2), (3, 2)), ((0, 2), (1, 1)),
                 ((1, 3), (3, 1)), ((3, 3), (1, 0)), ((3, 0), (0, 1)), ((0, 3), (0, 0))]
        for two in pairs:
            slots = [row_of(0, x + a, y + b) for a, b in two]
            right = jnp.concatenate([wd[l, p].reshape(8 * B, B) for p in slots], axis=1)
            value = dot(left, right).astype(BF16)
            for s, (a, b) in enumerate(two):
                for h in range(2):
                    du, dv = (a, b) if h == 0 else (b, a)
                    part_out[t, h, du, dv] = value[h * B:(h + 1) * B, s * B:(s + 1) * B]
                    if du:
                        part_copy(t, h, du, dv).start()
        keep = []
        for dv in (2, 1, 3, 0):
            for h in range(2):
                total = part_out[t, h, 0, dv].astype(F32)
                for du in (1, 3, 2):
                    part_copy(t, h, du, dv).wait_recv()
                    total = total + part_in[t, h, du, dv].astype(F32)
                if dv:
                    line_out[t, h, dv] = total.astype(BF16)
                    line_copy(t, h, dv).start()
                else:
                    keep.append(total)
        for h in range(2):
            for dv in (1, 3, 2):
                line_copy(t, h, dv).wait_recv()
                keep[h] = keep[h] + line_in[t, h, dv].astype(F32)
        residual_t = solved_t[l] - jnp.concatenate(keep, axis=0)
        sol_t = finish(l, t + 1, residual_t)
        out_ref[l] = sol_t.astype(F32).T.astype(BF16)
        return carry

    lax.fori_loop(0, 3, up, 0)

    def drain(l, carry):
        for h in range(2):
            for idx in range(15):
                gather_copy(l, h, row, idx, (row, col)).wait_send()
            for du in range(1, 4):
                for dv in range(4):
                    part_copy(l, h, du, dv).wait_send()
            for dv in range(1, 4):
                line_copy(l, h, dv).wait_send()
        for s in range(4):
            remote(sib_out.at[l, s], sib_in.at[l, s], sib_s.at[l, s], sib_r.at[l, s], sibling).wait_send()
            forward_copy(l, s).wait_send()
        for d in range(1, 4):
            remote(z_out.at[l, d - 1], z_in.at[l, d - 1], z_s.at[l, d - 1], z_r.at[l, d - 1], z_peer(d)).wait_send()
            up_copy(l, d).wait_send()
        return carry

    lax.fori_loop(0, 3, drain, 0)


def solve(ordered, diag, mask, lower):
    vmem = pl.BlockSpec(memory_space=pltpu.VMEM)
    dma = pltpu.SemaphoreType.DMA
    return pl.pallas_call(
        solve_kernel,
        out_shape=jax.ShapeDtypeStruct((NLEV, B, N), BF16),
        in_specs=[vmem, vmem, pl.BlockSpec(memory_space=pltpu.SMEM), pl.BlockSpec(memory_space=pl.ANY)],
        out_specs=vmem,
        scratch_shapes=[
            pltpu.VMEM((3, 8, B, 16, B), BF16),
            pltpu.VMEM((3, 16, 2, 4, B, B), BF16),
            pltpu.VMEM((4, 2, 16, B, B), BF16),
            pltpu.VMEM((2, 4, B, N), F32),
            pltpu.VMEM((3, 4, B, N), BF16),
            pltpu.VMEM((3, 4, B, N), BF16),
            pltpu.VMEM((3, 3, B, N), BF16),
            pltpu.VMEM((3, 3, B, N), BF16),
            pltpu.VMEM((4, N, B), F32),
            pltpu.VMEM((4, 2, 4, N, B), BF16),
            pltpu.VMEM((3, 2, 4, 4, B, B), BF16),
            pltpu.VMEM((3, 2, 4, 4, B, B), BF16),
            pltpu.VMEM((3, 2, 4, B, B), BF16),
            pltpu.VMEM((3, 2, 4, B, B), BF16),
            dma((3,)), dma((3, 2, 15)), dma((3, 2, 15)), dma((3, 4)), dma((3, 4)), dma((3, 3)), dma((3, 3)),
            dma((3, 3)), dma((3, 3)), dma((3, 4)), dma((3, 4)),
            dma((3, 2, 4, 4)), dma((3, 2, 4, 4)), dma((3, 2, 4)), dma((3, 2, 4)),
        ],
        compiler_params=pltpu.CompilerParams(
            collective_id=0, has_side_effects=True, vmem_limit_bytes=60 * 1024 * 1024
        ),
    )(ordered, diag, mask, lower)


def per_device(rhs_rows, dest_row, diag_inverse, lower_blocks, block_mask):
    supernodes = 128
    local_rows, column_total = rhs_rows.shape
    group_rows = local_rows // supernodes
    owner_idx = dest_row // B % supernodes
    position = dest_row // (supernodes * B) * B + dest_row % B
    sort_order = jnp.argsort(owner_idx, stable=True)
    sending = rhs_rows[sort_order]
    places = position[sort_order]
    axes = ("row", "col")
    arrived = lax.all_to_all(
        sending.reshape(supernodes, group_rows, column_total).astype(BF16), axes, split_axis=0, concat_axis=0, tiled=True
    ).astype(F32)
    arrived_pos = lax.all_to_all(places.reshape(supernodes, group_rows), axes, split_axis=0, concat_axis=0, tiled=True)
    ordered = (
        jnp.zeros_like(rhs_rows).at[arrived_pos.reshape(local_rows)].set(arrived.reshape(local_rows, column_total))
    )
    ordered = ordered.reshape(NLEV, B, column_total)
    mask = block_mask.reshape(3, 128)
    return solve(ordered, diag_inverse[:, 0], mask, lower_blocks)[:, None]


def solution(mesh):
    in_specs = (
        P(("row", "col"), None),
        P(("row", "col")),
        P(None, ("row", "col"), None, None),
        P(None, "row", None, None, "col", None, None),
        P(None, "row", None, "col", None),
    )
    out_specs = P(None, ("row", "col"), None, None)
    return jax.shard_map(per_device, mesh=mesh, in_specs=in_specs, out_specs=out_specs, check_vma=False)
```

```python
import jax
import jax.numpy as jnp
from jax import lax
from jax.experimental import pallas as pl
from jax.experimental.pallas import tpu as pltpu
from jax.sharding import PartitionSpec as P

B = 128
NLEV = 4
N = 256
MESH = pl.DeviceIdType.MESH
F32 = jnp.float32
BF16 = jnp.bfloat16


def dot(a, b):
    return jnp.dot(a, b, preferred_element_type=F32)


def dot_rows(a, b):
    return lax.dot_general(a, b, (((1,), (1,)), ((), ())), preferred_element_type=F32)


def one_hot(condition):
    return jnp.where(condition, 1.0, 0.0).astype(BF16)


def iota(shape, axis):
    return lax.broadcasted_iota(jnp.int32, shape, axis)


def solve_kernel(
    rhs_ref, dest_ref, diag_ref, mask_ref, w_hbm, out_ref,
    rows_out, rows_in, meta_out, meta_in, meta_sib, mix_out, mix_in, ordered_ref, raw, wd, gath, acc, sib_out, sib_in, z_out, z_in, solved_t, upper, part_out, part_in, line_out, line_in,
    rows_s, rows_r, meta_s, meta_r, mix_s, mix_r, load_sem, ag_s, ag_r, sib_s, sib_r, z_s, z_r, up_s, up_r, fw_s, fw_r, p1_s, p1_r, p2_s, p2_r,
):
    row = lax.axis_index("row")
    col = lax.axis_index("col")
    x, y = row // 4, row % 4
    z, core = col // 2, col % 2
    other = 1 - core

    def row_of(h, u, v):
        return (u % 4) * 4 + v % 4 if h == 0 else (v % 4) * 4 + u % 4

    first = (x, y)
    second = (y, x)

    def remote(src, dst, ssem, rsem, dev):
        return pltpu.make_async_remote_copy(
            src_ref=src, dst_ref=dst, send_sem=ssem, recv_sem=rsem, device_id=dev, device_id_type=MESH
        )

    sibling = (row, z * 2 + other)

    def z_peer(d):
        return (row, ((z + d) % 4) * 2 + core)

    chip = row * 4 + z

    def chip_peer(k):
        t = (chip + k) % 64
        return t, (t // 4, (t % 4) * 2 + core)

    barrier = pltpu.get_barrier_semaphore()
    pl.semaphore_signal(barrier, inc=1, device_id=sibling, device_id_type=MESH)

    def greet(k, carry):
        pl.semaphore_signal(barrier, inc=1, device_id=chip_peer(k)[1], device_id_type=MESH)
        return carry

    lax.fori_loop(1, 64, greet, 0)

    loads = [pltpu.make_async_copy(w_hbm.at[l, 0, :, :, 0], raw.at[l], load_sem.at[l]) for l in range(3)]
    for load in loads:
        load.start()

    def loads_wait(l):
        pltpu.make_async_copy(w_hbm.at[l, 0, :, :, 0], raw.at[l], load_sem.at[l]).wait()

    out_row, in_row = iota((256, 256), 0), iota((256, 256), 1)
    perm = one_hot(in_row == (out_row & 15) * 16 + (out_row >> 4))

    def relayout(l):
        def one(i, carry):
            zz, cc = i // 2, i % 2
            scale = [mask_ref[l, 0, i, 0, p].astype(F32) for p in range(16)]
            for k0 in range(0, 8, 2):
                piece = jnp.concatenate(
                    [raw[l, i, (k0 + s) * 16:(k0 + s + 1) * 16].reshape(256, B) for s in range(2)], axis=1
                )
                moved = dot(perm, piece)
                for p in range(16):
                    for s in range(2):
                        tile = moved[p * 16:(p + 1) * 16, s * B:(s + 1) * B] * scale[p]
                        wd[l, p, cc, zz, (k0 + s) * 16:(k0 + s + 1) * 16, :] = tile.astype(BF16)
            return carry

        lax.fori_loop(0, 8, one, 0)

    def put_solved(l, residual):
        solved = dot(diag_ref[l], residual).astype(BF16)
        return solved

    dest = dest_ref[...]
    owner = (dest >> 7) & 127
    place = (dest >> 14) * B + (dest & 127)
    owned = one_hot(iota((128, 512), 0) == owner)
    before = dot(owned, one_hot(iota((512, 512), 0) < iota((512, 512), 1)))
    rank = jnp.sum(owned.astype(F32) * before, axis=0, keepdims=True)
    slot = owner * 4 + rank.astype(jnp.int32)
    sort = one_hot(iota((512, 512), 0) == slot)
    rows_out[...] = dot(sort, rhs_ref[...].astype(BF16)).astype(BF16).reshape(64, 8, N)
    lane = iota((128, 512), 0)
    digit = jnp.where(lane < 8, place >> 4, place & 15)
    digit = jnp.where((lane < 16) & ((lane & 7) == (slot & 7)), digit, 0).astype(F32).astype(BF16)
    meta_out[...] = dot_rows(one_hot(iota((64, 512), 0) == (slot >> 3)), digit).reshape(64, 1, B)

    def rows_copy(t, dev):
        return remote(rows_out.at[t], rows_in.at[chip], rows_s, rows_r, dev)

    def meta_copy(t, dev):
        return remote(meta_out.at[t], meta_in.at[chip], meta_s, meta_r, dev)

    pl.semaphore_wait(barrier, 64)

    def send_rows(k, carry):
        t, dev = chip_peer(k)
        meta_copy(t, dev).start()
        rows_copy(t, dev).start()
        return carry

    lax.fori_loop(1, 64, send_rows, 0)
    rows_in[chip] = rows_out[chip]
    meta_in[chip] = meta_out[chip]

    def prepare(l, carry):
        loads_wait(l)
        relayout(l)
        return carry

    lax.fori_loop(0, 3, prepare, 0)

    some = pl.ds(0, 63)
    all_rows = remote(rows_out.at[some], rows_in.at[some], rows_s, rows_r, sibling)
    all_meta = remote(meta_out.at[some], meta_in.at[some], meta_s, meta_r, sibling)
    all_meta.wait_recv()
    meta_swap = remote(meta_in, meta_sib, mix_s.at[0], mix_r.at[0], sibling)
    meta_swap.start()
    all_rows.wait_recv()
    to, at = iota((512, 512), 0), iota((512, 512), 1)
    half = jnp.where(to < 256, core, other)
    mixed = dot(one_hot(at == (to & 63) * 8 + half * 4 + ((to >> 6) & 3)), rows_in[...].reshape(512, N)).astype(BF16)
    mix_out[...] = mixed[256:]
    mix_swap = remote(mix_out, mix_in, mix_s.at[1], mix_r.at[1], sibling)
    mix_swap.start()

    def place_rows(meta, rows):
        digits = jnp.concatenate([meta.reshape(64, B)] * 4, axis=0)
        at_lane, k = iota((256, B), 1), iota((256, B), 0) >> 6
        mine = (at_lane < 16) & ((at_lane & 7) == core * 4 + k)
        weight = jnp.where(iota((8, B), 1) < 8, 16.0, 1.0).astype(BF16)
        where = dot_rows(weight, jnp.where(mine, digits, 0.0).astype(BF16))[:1]
        return dot(one_hot(iota((512, 256), 0) == where.astype(jnp.int32)), rows)

    total = place_rows(meta_in[...], mixed[:256])
    meta_swap.wait_recv()
    mix_swap.wait_recv()
    ordered_ref[...] = (total + place_rows(meta_sib[...], mix_in[...])).reshape(NLEV, B, N)

    level0 = put_solved(0, ordered_ref[0].astype(BF16))
    gath[0, 0, row] = level0[:, :B]
    gath[0, 1, row] = level0[:, B:]
    solved_t[0] = level0.astype(F32).T

    def gather_copy(l, h, slot, idx, dev):
        return remote(gath.at[l, h, slot], gath.at[l, h, slot], ag_s.at[l, h, idx], ag_r.at[l, h, idx], dev)

    def pair_rhs(l, p):
        return jnp.concatenate([gath[l, 0, p], gath[l, 1, p]], axis=1)

    def down(l, carry):
        for h in range(2):
            u, v = first if h == 0 else second
            for d in (2, 1, 3):
                gather_copy(l, h, row, d - 1, (row_of(h, u + d, v), col)).start()
        for e in (0, 1, 3, 2):
            for h in range(2):
                u, v = first if h == 0 else second
                slot = row_of(h, u - e, v)
                if e:
                    gather_copy(l, h, slot, e - 1, (row, col)).wait_recv()
                for d in (2, 1, 3):
                    gather_copy(l, h, slot, 3 + e * 3 + d - 1, (row_of(h, u, v + d), col)).start()
        order = [(a, b) for a in (0, 1, 3) for b in (0, 1, 3)] + [(a, b) for a in range(4) for b in range(4) if 2 in (a, b)]
        done = set()

        def arrive(a, b):
            for h in range(2):
                e, d = (a, b) if h == 0 else (b, a)
                u, v = first if h == 0 else second
                if d and (h, e, d) not in done:
                    done.add((h, e, d))
                    gather_copy(l, h, row_of(h, u - e, v - d), 3 + e * 3 + d - 1, (row, col)).wait_recv()

        def operands(some):
            slots = [row_of(0, x - a, y - b) for a, b in some]
            rhs = jnp.concatenate([pair_rhs(l, p) for p in slots], axis=0)
            return slots, rhs

        def lhs(slots, c, r, n):
            return jnp.concatenate([wd[l, p, c, r:r + n].reshape(n * B, B) for p in slots], axis=1)

        for a, b in order[:8]:
            arrive(a, b)
        slots, rhs = operands(order[:8])
        for c in range(2):
            for r in range(0, 4, 2):
                acc[c, r:r + 2] = dot(lhs(slots, c, r, 2), rhs).reshape(2, B, N)
        for a, b in order[8:]:
            arrive(a, b)
        slots, rhs = operands(order[8:])
        for step, c in enumerate((other, core)):
            for half in range(2):
                r = ((z // 2 + 1 - half) % 2) * 2
                left = jnp.concatenate([wd[l, p, c, pl.ds(r, 2)].reshape(2 * B, B) for p in slots], axis=1)
                total = acc[c, pl.ds(r, 2)] + dot(left, rhs).reshape(2, B, N)
                if step == 0:
                    sib_out[l, pl.ds(r, 2)] = total.astype(BF16)
                    for s in range(2):
                        remote(sib_out.at[l, r + s], sib_in.at[l, r + s], sib_s.at[l, half * 2 + s], sib_r.at[l, r + s], sibling).start()
                else:
                    acc[c, pl.ds(r, 2)] = total
        for d in (2, 1, 3, 0):
            zz = (z + d) % 4
            remote(sib_out.at[l, zz], sib_in.at[l, zz], sib_s.at[l, 0], sib_r.at[l, zz], sibling).wait_recv()
            total = acc[core, zz] + sib_in[l, zz].astype(F32)
            if d:
                z_out[l, d - 1] = total.astype(BF16)
                remote(z_out.at[l, d - 1], z_in.at[l, d - 1], z_s.at[l, d - 1], z_r.at[l, d - 1], z_peer(d)).start()
            else:
                own = total
        for d in (1, 3, 2):
            remote(z_out.at[l, d - 1], z_in.at[l, d - 1], z_s.at[l, d - 1], z_r.at[l, d - 1], z_peer(d)).wait_recv()
            own = own + z_in[l, d - 1].astype(F32)
        residual = (ordered_ref[l + 1] - own).astype(BF16)
        solved = put_solved(l + 1, residual)
        gath[l + 1, 0, row] = solved[:, :B]
        gath[l + 1, 1, row] = solved[:, B:]
        solved_t[l + 1] = solved.astype(F32).T
        return carry

    lax.fori_loop(0, 3, down, 0)

    def finish(l, slot, residual_t):
        sol_t = dot(residual_t.astype(BF16), diag_ref[l]).astype(BF16)
        upper[slot, core, z] = sol_t
        return sol_t

    top = finish(3, 0, solved_t[3])
    out_ref[3] = top.astype(F32).T.astype(BF16)

    def up_copy(t, d):
        return remote(upper.at[t, core, z], upper.at[t, core, z], up_s.at[t, d - 1], up_r.at[t, d - 1], z_peer(d))

    def forward_copy(t, d):
        slot = upper.at[t, core, (z - d) % 4]
        return remote(slot, slot, fw_s.at[t, d], fw_r.at[t, d], sibling)

    def part_copy(t, h, du, dv):
        u, v = first if h == 0 else second
        return remote(
            part_out.at[t, h, du, dv], part_in.at[t, h, du, dv],
            p1_s.at[t, h, du, dv], p1_r.at[t, h, du, dv], (row_of(h, u + du, v), col),
        )

    def line_copy(t, h, dv):
        u, v = first if h == 0 else second
        return remote(
            line_out.at[t, h, dv], line_in.at[t, h, dv], p2_s.at[t, h, dv], p2_r.at[t, h, dv], (row_of(h, u, v + dv), col)
        )

    def up(t, carry):
        l = 2 - t
        for d in (2, 1, 3):
            up_copy(t, d).start()
        forward_copy(t, 0).start()
        for d in (1, 3, 2):
            slot = upper.at[t, core, (z - d) % 4]
            remote(slot, slot, up_s.at[t, d - 1], up_r.at[t, d - 1], sibling).wait_recv()
            forward_copy(t, d).start()
        for d in (0, 1, 3, 2):
            slot = upper.at[t, other, (z - d) % 4]
            remote(slot, slot, fw_s.at[t, d], fw_r.at[t, d], sibling).wait_recv()
        left = jnp.concatenate([upper[t, c, r] for c in range(2) for r in range(4)], axis=1)
        pairs = [((2, 2), (2, 1)), ((2, 3), (2, 0)), ((1, 2), (3, 2)), ((0, 2), (1, 1)),
                 ((1, 3), (3, 1)), ((3, 3), (1, 0)), ((3, 0), (0, 1)), ((0, 3), (0, 0))]
        for two in pairs:
            slots = [row_of(0, x + a, y + b) for a, b in two]
            right = jnp.concatenate([wd[l, p].reshape(8 * B, B) for p in slots], axis=1)
            value = dot(left, right).astype(BF16)
            for s, (a, b) in enumerate(two):
                for h in range(2):
                    du, dv = (a, b) if h == 0 else (b, a)
                    part_out[t, h, du, dv] = value[h * B:(h + 1) * B, s * B:(s + 1) * B]
                    if du:
                        part_copy(t, h, du, dv).start()
        keep = []
        for dv in (2, 1, 3, 0):
            for h in range(2):
                total = part_out[t, h, 0, dv].astype(F32)
                for du in (1, 3, 2):
                    part_copy(t, h, du, dv).wait_recv()
                    total = total + part_in[t, h, du, dv].astype(F32)
                if dv:
                    line_out[t, h, dv] = total.astype(BF16)
                    line_copy(t, h, dv).start()
                else:
                    keep.append(total)
        for h in range(2):
            for dv in (1, 3, 2):
                line_copy(t, h, dv).wait_recv()
                keep[h] = keep[h] + line_in[t, h, dv].astype(F32)
        residual_t = solved_t[l] - jnp.concatenate(keep, axis=0)
        sol_t = finish(l, t + 1, residual_t)
        out_ref[l] = sol_t.astype(F32).T.astype(BF16)
        return carry

    lax.fori_loop(0, 3, up, 0)

    def drain(l, carry):
        for h in range(2):
            for idx in range(15):
                gather_copy(l, h, row, idx, (row, col)).wait_send()
            for du in range(1, 4):
                for dv in range(4):
                    part_copy(l, h, du, dv).wait_send()
            for dv in range(1, 4):
                line_copy(l, h, dv).wait_send()
        for s in range(4):
            remote(sib_out.at[l, s], sib_in.at[l, s], sib_s.at[l, s], sib_r.at[l, s], sibling).wait_send()
            forward_copy(l, s).wait_send()
        for d in range(1, 4):
            remote(z_out.at[l, d - 1], z_in.at[l, d - 1], z_s.at[l, d - 1], z_r.at[l, d - 1], z_peer(d)).wait_send()
            up_copy(l, d).wait_send()
        return carry

    lax.fori_loop(0, 3, drain, 0)
    all_rows.wait_send()
    all_meta.wait_send()
    meta_swap.wait_send()
    mix_swap.wait_send()


def solve(rhs, dest, diag, mask, lower):
    vmem = pl.BlockSpec(memory_space=pltpu.VMEM)
    dma = pltpu.SemaphoreType.DMA
    return pl.pallas_call(
        solve_kernel,
        out_shape=jax.ShapeDtypeStruct((NLEV, B, N), BF16),
        in_specs=[vmem, vmem, vmem, pl.BlockSpec(memory_space=pltpu.SMEM), pl.BlockSpec(memory_space=pl.ANY)],
        out_specs=vmem,
        scratch_shapes=[
            pltpu.VMEM((64, 8, N), BF16),
            pltpu.VMEM((64, 8, N), BF16),
            pltpu.VMEM((64, 1, B), F32),
            pltpu.VMEM((64, 1, B), F32),
            pltpu.VMEM((64, 1, B), F32),
            pltpu.VMEM((256, N), BF16),
            pltpu.VMEM((256, N), BF16),
            pltpu.VMEM((NLEV, B, N), F32),
            pltpu.VMEM((3, 8, B, 16, B), BF16),
            pltpu.VMEM((3, 16, 2, 4, B, B), BF16),
            pltpu.VMEM((4, 2, 16, B, B), BF16),
            pltpu.VMEM((2, 4, B, N), F32),
            pltpu.VMEM((3, 4, B, N), BF16),
            pltpu.VMEM((3, 4, B, N), BF16),
            pltpu.VMEM((3, 3, B, N), BF16),
            pltpu.VMEM((3, 3, B, N), BF16),
            pltpu.VMEM((4, N, B), F32),
            pltpu.VMEM((4, 2, 4, N, B), BF16),
            pltpu.VMEM((3, 2, 4, 4, B, B), BF16),
            pltpu.VMEM((3, 2, 4, 4, B, B), BF16),
            pltpu.VMEM((3, 2, 4, B, B), BF16),
            pltpu.VMEM((3, 2, 4, B, B), BF16),
            dma, dma, dma, dma, dma((2,)), dma((2,)),
            dma((3,)), dma((3, 2, 15)), dma((3, 2, 15)), dma((3, 4)), dma((3, 4)), dma((3, 3)), dma((3, 3)),
            dma((3, 3)), dma((3, 3)), dma((3, 4)), dma((3, 4)),
            dma((3, 2, 4, 4)), dma((3, 2, 4, 4)), dma((3, 2, 4)), dma((3, 2, 4)),
        ],
        compiler_params=pltpu.CompilerParams(
            collective_id=0, has_side_effects=True, vmem_limit_bytes=60 * 1024 * 1024
        ),
    )(rhs, dest, diag, mask, lower)


def per_device(rhs_rows, dest_row, diag_inverse, lower_blocks, block_mask):
    dest = dest_row.reshape(1, dest_row.shape[0])
    return solve(rhs_rows, dest, diag_inverse[:, 0], block_mask, lower_blocks)[:, None]


def solution(mesh):
    in_specs = (
        P(("row", "col"), None),
        P(("row", "col")),
        P(None, ("row", "col"), None, None),
        P(None, "row", None, None, "col", None, None),
        P(None, "row", None, "col", None),
    )
    out_specs = P(None, ("row", "col"), None, None)
    return jax.shard_map(per_device, mesh=mesh, in_specs=in_specs, out_specs=out_specs, check_vma=False)
```

```python
import jax
import jax.numpy as jnp
from jax import lax
from jax.experimental import pallas as pl
from jax.experimental.pallas import tpu as pltpu
from jax.sharding import PartitionSpec as P

B = 128
NLEV = 4
N = 256
MESH = pl.DeviceIdType.MESH
F32 = jnp.float32
BF16 = jnp.bfloat16


def dot(a, b):
    return jnp.dot(a, b, preferred_element_type=F32)


def dot_rows(a, b):
    return lax.dot_general(a, b, (((1,), (1,)), ((), ())), preferred_element_type=F32)


def one_hot(condition):
    return jnp.where(condition, 1.0, 0.0).astype(BF16)


def iota(shape, axis):
    return lax.broadcasted_iota(jnp.int32, shape, axis)


def solve_kernel(
    rhs_ref, dest_ref, diag_ref, mask_ref, w_hbm, out_hbm,
    hello, out_ref,     rows_out, rows_in, meta_out, meta_in, meta_sib, mix_out, mix_in, ordered_ref, raw, wd, gath, acc, sib_out, sib_in, z_out, z_in, solved_t, upper, part_out, part_in, line_out, line_in,
    rows_s, rows_r, meta_s, meta_r, mix_s, mix_r, load_sem, out_sem, ag_s, ag_r, sib_s, sib_r, z_s, z_r, up_s, up_r, fw_s, fw_r, p1_s, p1_r, p2_s, p2_r,
):
    row = lax.axis_index("row")
    col = lax.axis_index("col")
    x, y = row // 4, row % 4
    z, core = col // 2, col % 2
    other = 1 - core

    def row_of(h, u, v):
        return (u % 4) * 4 + v % 4 if h == 0 else (v % 4) * 4 + u % 4

    first = (x, y)
    second = (y, x)

    def remote(src, dst, ssem, rsem, dev):
        return pltpu.make_async_remote_copy(
            src_ref=src, dst_ref=dst, send_sem=ssem, recv_sem=rsem, device_id=dev, device_id_type=MESH
        )

    sibling = (row, z * 2 + other)

    def z_peer(d):
        return (row, ((z + d) % 4) * 2 + core)

    chip = row * 4 + z

    def chip_peer(k):
        t = (chip + k) % 64
        return t, (t // 4, (t % 4) * 2 + core)

    def line(axis):
        if axis == "x":
            return [(row_of(0, x + d, y), col) for d in (1, 2, 3)]
        return [(row_of(0, x, y + d), col) for d in (1, 2, 3)]

    near = [(row_of(0, x + a, y), ((z + b) % 4) * 2 + core) for a in range(4) for b in range(4) if a or b]
    near += line("y") + [sibling]
    barrier = pltpu.get_barrier_semaphore()
    for dev in near:
        pl.semaphore_signal(barrier, inc=1, device_id=dev, device_id_type=MESH)

    loads = [pltpu.make_async_copy(w_hbm.at[l, 0, :, :, 0], raw.at[l], load_sem.at[l]) for l in range(3)]
    for load in loads:
        load.start()

    def loads_wait(l):
        pltpu.make_async_copy(w_hbm.at[l, 0, :, :, 0], raw.at[l], load_sem.at[l]).wait()

    out_row, in_row = iota((256, 256), 0), iota((256, 256), 1)
    perm = one_hot(in_row == (out_row & 15) * 16 + (out_row >> 4))

    def relayout(l):
        def one(i, carry):
            zz, cc = i // 2, i % 2
            scale = [mask_ref[l, 0, i, 0, p].astype(F32) for p in range(16)]
            for k0 in range(0, 8, 2):
                piece = jnp.concatenate(
                    [raw[l, i, (k0 + s) * 16:(k0 + s + 1) * 16].reshape(256, B) for s in range(2)], axis=1
                )
                moved = dot(perm, piece)
                for p in range(16):
                    for s in range(2):
                        tile = moved[p * 16:(p + 1) * 16, s * B:(s + 1) * B] * scale[p]
                        wd[l, p, cc, zz, (k0 + s) * 16:(k0 + s + 1) * 16, :] = tile.astype(BF16)
            return carry

        lax.fori_loop(0, 8, one, 0)

    def put_solved(l, residual):
        solved = dot(diag_ref[l], residual).astype(BF16)
        return solved

    def prepare(l, carry):
        loads_wait(l)
        relayout(l)
        return carry

    dest = dest_ref[...]
    owner = (dest >> 7) & 127
    place = (dest >> 14) * B + (dest & 127)
    owned = one_hot(iota((128, 512), 0) == owner)
    before = dot(owned, one_hot(iota((512, 512), 0) < iota((512, 512), 1)))
    rank = jnp.sum(owned.astype(F32) * before, axis=0, keepdims=True)
    slot = owner * 4 + rank.astype(jnp.int32)
    sort = one_hot(iota((512, 512), 0) == slot)
    rows_out[...] = dot(sort, rhs_ref[...].astype(BF16)).astype(BF16).reshape(64, 8, N)
    lane = iota((128, 512), 0)
    digit = jnp.where(lane < 8, place >> 4, place & 15)
    digit = jnp.where((lane < 16) & ((lane & 7) == (slot & 7)), digit, 0).astype(F32).astype(BF16)
    meta_out[...] = dot_rows(one_hot(iota((64, 512), 0) == (slot >> 3)), digit).reshape(64, 1, B)

    def rows_copy(t, dev):
        return remote(rows_out.at[t], rows_in.at[chip], rows_s, rows_r, dev)

    def meta_copy(t, dev):
        return remote(meta_out.at[t], meta_in.at[chip], meta_s, meta_r, dev)

    pl.semaphore_wait(barrier, len(near))
    for dev in line("y"):
        pl.semaphore_signal(hello, inc=1, device_id=dev, device_id_type=MESH)
    prepare(0, 0)
    pl.semaphore_wait(hello, 3)

    def send_rows(k, carry):
        t, dev = chip_peer(k)
        meta_copy(t, dev).start()
        rows_copy(t, dev).start()
        return carry

    lax.fori_loop(1, 64, send_rows, 0)
    rows_in[chip] = rows_out[chip]
    meta_in[chip] = meta_out[chip]

    lax.fori_loop(1, 3, prepare, 0)

    some = pl.ds(0, 63)
    all_rows = remote(rows_out.at[some], rows_in.at[some], rows_s, rows_r, sibling)
    all_meta = remote(meta_out.at[some], meta_in.at[some], meta_s, meta_r, sibling)
    all_meta.wait_recv()
    meta_swap = remote(meta_in, meta_sib, mix_s.at[0], mix_r.at[0], sibling)
    meta_swap.start()
    all_rows.wait_recv()
    to, at = iota((512, 512), 0), iota((512, 512), 1)
    half = jnp.where(to < 256, core, other)
    mixed = dot(one_hot(at == (to & 63) * 8 + half * 4 + ((to >> 6) & 3)), rows_in[...].reshape(512, N)).astype(BF16)
    mix_out[...] = mixed[256:]
    mix_swap = remote(mix_out, mix_in, mix_s.at[1], mix_r.at[1], sibling)
    mix_swap.start()

    def place_rows(meta, rows):
        digits = jnp.concatenate([meta.reshape(64, B)] * 4, axis=0)
        at_lane, k = iota((256, B), 1), iota((256, B), 0) >> 6
        mine = (at_lane < 16) & ((at_lane & 7) == core * 4 + k)
        weight = jnp.where(iota((8, B), 1) < 8, 16.0, 1.0).astype(BF16)
        where = dot_rows(weight, jnp.where(mine, digits, 0.0).astype(BF16))[:1]
        return dot(one_hot(iota((512, 256), 0) == where.astype(jnp.int32)), rows)

    total = place_rows(meta_in[...], mixed[:256])
    meta_swap.wait_recv()
    mix_swap.wait_recv()
    ordered_ref[...] = (total + place_rows(meta_sib[...], mix_in[...])).reshape(NLEV, B, N)

    level0 = put_solved(0, ordered_ref[0].astype(BF16))
    gath[0, 0, row] = level0[:, :B]
    gath[0, 1, row] = level0[:, B:]
    solved_t[0] = level0.astype(F32).T

    def gather_copy(l, h, slot, idx, dev):
        return remote(gath.at[l, h, slot], gath.at[l, h, slot], ag_s.at[l, h, idx], ag_r.at[l, h, idx], dev)

    def pair_rhs(l, p):
        return jnp.concatenate([gath[l, 0, p], gath[l, 1, p]], axis=1)

    def down(l, carry):
        def send(h, e, d, relay):
            u, v = first if h == 0 else second
            slot = row_of(h, u - e, v) if relay else row
            target = row_of(h, u if relay else u + e, v + d)
            gather_copy(l, h, slot, e - 1 if d == 0 else 3 + e * 3 + d - 1, (target, col)).start()

        for e, d in ((1, 0), (3, 0), (0, 2), (0, 1), (0, 3), (2, 0), (2, 2), (2, 1), (2, 3)):
            for h in range(2):
                send(h, e, d, False)
        for e in (1, 3):
            for h in range(2):
                u, v = first if h == 0 else second
                gather_copy(l, h, row_of(h, u - e, v), e - 1, (row, col)).wait_recv()
                for d in (2, 1, 3):
                    send(h, e, d, True)
        order = [(0, 0), (0, 1), (0, 3), (1, 0), (3, 0), (0, 2), (2, 0), (2, 2), (1, 1), (1, 3), (3, 1), (3, 3), (1, 2), (2, 1), (2, 3), (3, 2)]
        batches = [order[:8], order[8:12], order[12:]]

        def arrive(a, b):
            for h in range(2):
                e, d = (a, b) if h == 0 else (b, a)
                u, v = first if h == 0 else second
                if d or e == 2:
                    index = 3 + e * 3 + d - 1 if d else e - 1
                    gather_copy(l, h, row_of(h, u - e, v - d), index, (row, col)).wait_recv()

        def operands(some):
            slots = [row_of(0, x - a, y - b) for a, b in some]
            rhs = jnp.concatenate([pair_rhs(l, p) for p in slots], axis=0)
            return slots, rhs

        def lhs(slots, c, r, n):
            return jnp.concatenate([wd[l, p, c, r:r + n].reshape(n * B, B) for p in slots], axis=1)

        for index, batch in enumerate(batches):
            for a, b in batch:
                arrive(a, b)
            slots, rhs = operands(batch)
            if index == 2:
                break
            for c in range(2):
                for r in range(0, 4, 2):
                    part = dot(lhs(slots, c, r, 2), rhs).reshape(2, B, N)
                    acc[c, r:r + 2] = part if index == 0 else acc[c, r:r + 2] + part
        for step, c in enumerate((other, core)):
            for half in range(2):
                r = ((z // 2 + 1 - half) % 2) * 2
                left = jnp.concatenate([wd[l, p, c, pl.ds(r, 2)].reshape(2 * B, B) for p in slots], axis=1)
                total = acc[c, pl.ds(r, 2)] + dot(left, rhs).reshape(2, B, N)
                if step == 0:
                    sib_out[l, pl.ds(r, 2)] = total.astype(BF16)
                    for s in range(2):
                        remote(sib_out.at[l, r + s], sib_in.at[l, r + s], sib_s.at[l, half * 2 + s], sib_r.at[l, r + s], sibling).start()
                else:
                    acc[c, pl.ds(r, 2)] = total
        for d in (2, 1, 3, 0):
            zz = (z + d) % 4
            remote(sib_out.at[l, zz], sib_in.at[l, zz], sib_s.at[l, 0], sib_r.at[l, zz], sibling).wait_recv()
            total = acc[core, zz] + sib_in[l, zz].astype(F32)
            if d:
                z_out[l, d - 1] = total.astype(BF16)
                remote(z_out.at[l, d - 1], z_in.at[l, d - 1], z_s.at[l, d - 1], z_r.at[l, d - 1], z_peer(d)).start()
            else:
                own = total
        for d in (1, 3, 2):
            remote(z_out.at[l, d - 1], z_in.at[l, d - 1], z_s.at[l, d - 1], z_r.at[l, d - 1], z_peer(d)).wait_recv()
            own = own + z_in[l, d - 1].astype(F32)
        residual = (ordered_ref[l + 1] - own).astype(BF16)
        solved = put_solved(l + 1, residual)
        gath[l + 1, 0, row] = solved[:, :B]
        gath[l + 1, 1, row] = solved[:, B:]
        solved_t[l + 1] = solved.astype(F32).T
        return carry

    lax.fori_loop(0, 3, down, 0)

    def finish(l, slot, residual_t):
        sol_t = dot(residual_t.astype(BF16), diag_ref[l]).astype(BF16)
        upper[slot, core, z] = sol_t
        return sol_t

    def out_copy(l):
        return pltpu.make_async_copy(out_ref.at[l], out_hbm.at[l], out_sem.at[l])

    def emit(l, sol_t):
        out_ref[l] = sol_t.astype(F32).T.astype(BF16)
        out_copy(l).start()

    top = finish(3, 0, solved_t[3])
    emit(3, top)

    def up_copy(t, d):
        return remote(upper.at[t, core, z], upper.at[t, core, z], up_s.at[t, d - 1], up_r.at[t, d - 1], z_peer(d))

    def forward_copy(t, d):
        slot = upper.at[t, core, (z - d) % 4]
        return remote(slot, slot, fw_s.at[t, d], fw_r.at[t, d], sibling)

    def part_copy(t, h, du, dv):
        u, v = first if h == 0 else second
        return remote(
            part_out.at[t, h, du, dv], part_in.at[t, h, du, dv],
            p1_s.at[t, h, du, dv], p1_r.at[t, h, du, dv], (row_of(h, u + du, v + dv if du == 2 else v), col),
        )

    def line_copy(t, h, dv):
        u, v = first if h == 0 else second
        return remote(
            line_out.at[t, h, dv], line_in.at[t, h, dv], p2_s.at[t, h, dv], p2_r.at[t, h, dv], (row_of(h, u, v + dv), col)
        )

    def up(t, carry):
        l = 2 - t
        for d in (2, 1, 3):
            up_copy(t, d).start()
        forward_copy(t, 0).start()
        for d in (1, 3, 2):
            slot = upper.at[t, core, (z - d) % 4]
            remote(slot, slot, up_s.at[t, d - 1], up_r.at[t, d - 1], sibling).wait_recv()
            forward_copy(t, d).start()
        for d in (0, 1, 3, 2):
            slot = upper.at[t, other, (z - d) % 4]
            remote(slot, slot, fw_s.at[t, d], fw_r.at[t, d], sibling).wait_recv()
        left = jnp.concatenate([upper[t, c, r] for c in range(2) for r in range(4)], axis=1)
        pairs = [((1, 1), (1, 3)), ((3, 1), (3, 3)), ((1, 2), (3, 2)), ((2, 1), (2, 3)),
                 ((2, 2), (0, 2)), ((2, 0), (0, 1)), ((1, 0), (0, 3)), ((3, 0), (0, 0))]
        later = []
        for index, two in enumerate(pairs):
            slots = [row_of(0, x + a, y + b) for a, b in two]
            right = jnp.concatenate([wd[l, p].reshape(8 * B, B) for p in slots], axis=1)
            value = dot(left, right).astype(BF16)
            for s, (a, b) in enumerate(two):
                for h in range(2):
                    du, dv = (a, b) if h == 0 else (b, a)
                    part_out[t, h, du, dv] = value[h * B:(h + 1) * B, s * B:(s + 1) * B]
                    if du == 2 and index < 4:
                        later.append((h, du, dv))
                    elif du:
                        part_copy(t, h, du, dv).start()
            if index == 3:
                for h, du, dv in later:
                    part_copy(t, h, du, dv).start()

        def piece(h, du, dv):
            part_copy(t, h, du, dv).wait_recv()
            return part_in[t, h, du, dv].astype(F32)

        for dv in (2, 1, 3):
            for h in range(2):
                total = part_out[t, h, 0, dv].astype(F32) + piece(h, 1, dv) + piece(h, 3, dv)
                line_out[t, h, dv] = total.astype(BF16)
                line_copy(t, h, dv).start()
        keep = []
        for h in range(2):
            total = part_out[t, h, 0, 0].astype(F32)
            for du, dv in ((1, 0), (3, 0), (2, 0), (2, 1), (2, 3), (2, 2)):
                total = total + piece(h, du, dv)
            keep.append(total)
        for h in range(2):
            for dv in (1, 3, 2):
                line_copy(t, h, dv).wait_recv()
                keep[h] = keep[h] + line_in[t, h, dv].astype(F32)
        residual_t = solved_t[l] - jnp.concatenate(keep, axis=0)
        sol_t = finish(l, t + 1, residual_t)
        emit(l, sol_t)
        return carry

    lax.fori_loop(0, 3, up, 0)

    def drain_down(l, carry):
        for h in range(2):
            for idx in range(15):
                gather_copy(l, h, row, idx, (row, col)).wait_send()
        for s in range(4):
            remote(sib_out.at[l, s], sib_in.at[l, s], sib_s.at[l, s], sib_r.at[l, s], sibling).wait_send()
        for d in range(1, 4):
            remote(z_out.at[l, d - 1], z_in.at[l, d - 1], z_s.at[l, d - 1], z_r.at[l, d - 1], z_peer(d)).wait_send()
        return carry

    lax.fori_loop(0, 3, drain_down, 0)

    def drain_up(t, carry):
        for h in range(2):
            for du in range(1, 4):
                for dv in range(4):
                    part_copy(t, h, du, dv).wait_send()
            for dv in range(1, 4):
                line_copy(t, h, dv).wait_send()
        for d in range(4):
            forward_copy(t, d).wait_send()
            if d:
                up_copy(t, d).wait_send()
        return carry

    lax.fori_loop(0, 3, drain_up, 0)
    for l in range(NLEV):
        out_copy(l).wait()
    all_rows.wait_send()
    all_meta.wait_send()
    meta_swap.wait_send()
    mix_swap.wait_send()


def solve(rhs, dest, diag, mask, lower):
    vmem = pl.BlockSpec(memory_space=pltpu.VMEM)
    dma = pltpu.SemaphoreType.DMA
    return pl.pallas_call(
        solve_kernel,
        out_shape=jax.ShapeDtypeStruct((NLEV, B, N), BF16),
        in_specs=[vmem, vmem, vmem, pl.BlockSpec(memory_space=pltpu.SMEM), pl.BlockSpec(memory_space=pl.ANY)],
        out_specs=pl.BlockSpec(memory_space=pl.ANY),
        scratch_shapes=[
            pltpu.SemaphoreType.REGULAR,
            pltpu.VMEM((NLEV, B, N), BF16),
            pltpu.VMEM((64, 8, N), BF16),
            pltpu.VMEM((64, 8, N), BF16),
            pltpu.VMEM((64, 1, B), F32),
            pltpu.VMEM((64, 1, B), F32),
            pltpu.VMEM((64, 1, B), F32),
            pltpu.VMEM((256, N), BF16),
            pltpu.VMEM((256, N), BF16),
            pltpu.VMEM((NLEV, B, N), F32),
            pltpu.VMEM((3, 8, B, 16, B), BF16),
            pltpu.VMEM((3, 16, 2, 4, B, B), BF16),
            pltpu.VMEM((4, 2, 16, B, B), BF16),
            pltpu.VMEM((2, 4, B, N), F32),
            pltpu.VMEM((3, 4, B, N), BF16),
            pltpu.VMEM((3, 4, B, N), BF16),
            pltpu.VMEM((3, 3, B, N), BF16),
            pltpu.VMEM((3, 3, B, N), BF16),
            pltpu.VMEM((4, N, B), F32),
            pltpu.VMEM((4, 2, 4, N, B), BF16),
            pltpu.VMEM((3, 2, 4, 4, B, B), BF16),
            pltpu.VMEM((3, 2, 4, 4, B, B), BF16),
            pltpu.VMEM((3, 2, 4, B, B), BF16),
            pltpu.VMEM((3, 2, 4, B, B), BF16),
            dma, dma, dma, dma, dma((2,)), dma((2,)),
            dma((3,)), dma((NLEV,)), dma((3, 2, 15)), dma((3, 2, 15)), dma((3, 4)), dma((3, 4)), dma((3, 3)), dma((3, 3)),
            dma((3, 3)), dma((3, 3)), dma((3, 4)), dma((3, 4)),
            dma((3, 2, 4, 4)), dma((3, 2, 4, 4)), dma((3, 2, 4)), dma((3, 2, 4)),
        ],
        compiler_params=pltpu.CompilerParams(
            collective_id=0, has_side_effects=True, vmem_limit_bytes=50 * 1024 * 1024
        ),
    )(rhs, dest, diag, mask, lower)


def per_device(rhs_rows, dest_row, diag_inverse, lower_blocks, block_mask):
    dest = dest_row.reshape(1, dest_row.shape[0])
    return solve(rhs_rows, dest, diag_inverse[:, 0], block_mask, lower_blocks)[:, None]


def solution(mesh):
    in_specs = (
        P(("row", "col"), None),
        P(("row", "col")),
        P(None, ("row", "col"), None, None),
        P(None, "row", None, None, "col", None, None),
        P(None, "row", None, "col", None),
    )
    out_specs = P(None, ("row", "col"), None, None)
    return jax.shard_map(per_device, mesh=mesh, in_specs=in_specs, out_specs=out_specs, check_vma=False)
```

```python
import jax
import jax.numpy as jnp
from jax import lax
from jax.experimental import pallas as pl
from jax.experimental.pallas import tpu as pltpu
from jax.sharding import PartitionSpec as P

B = 128
NLEV = 4
N = 256
MESH = pl.DeviceIdType.MESH
F32 = jnp.float32
BF16 = jnp.bfloat16


def dot(a, b):
    return jnp.dot(a, b, preferred_element_type=F32)


def dot_rows(a, b):
    return lax.dot_general(a, b, (((1,), (1,)), ((), ())), preferred_element_type=F32)


def one_hot(condition):
    return jnp.where(condition, 1.0, 0.0).astype(BF16)


def iota(shape, axis):
    return lax.broadcasted_iota(jnp.int32, shape, axis)


def solve_kernel(
    rhs_hbm, dest_hbm, diag_hbm, mask_hbm, w_hbm, out_hbm,
    hello, rhs_ref, dest_ref, diag_ref, mask_ref, out_ref,     rows_out, rows_in, meta_out, meta_in, meta_sib, mix_out, mix_in, ordered_ref, raw, wd, gath, acc, sib_out, sib_in, z_out, z_in, solved_t, upper, part_out, part_in, line_out, line_in,
    rows_s, rows_r, meta_s, meta_r, mix_s, mix_r, in_sem, load_sem, out_sem, ag_s, ag_r, sib_s, sib_r, z_s, z_r, up_s, up_r, fw_s, fw_r, p1_s, p1_r, p2_s, p2_r,
):
    row = lax.axis_index("row")
    col = lax.axis_index("col")
    x, y = row // 4, row % 4
    z, core = col // 2, col % 2
    other = 1 - core

    def row_of(h, u, v):
        return (u % 4) * 4 + v % 4 if h == 0 else (v % 4) * 4 + u % 4

    first = (x, y)
    second = (y, x)

    def remote(src, dst, ssem, rsem, dev):
        return pltpu.make_async_remote_copy(
            src_ref=src, dst_ref=dst, send_sem=ssem, recv_sem=rsem, device_id=dev, device_id_type=MESH
        )

    sibling = (row, z * 2 + other)

    def z_peer(d):
        return (row, ((z + d) % 4) * 2 + core)

    chip = row * 4 + z

    def chip_peer(k):
        t = (chip + k) % 64
        return t, (t // 4, (t % 4) * 2 + core)

    def line(axis):
        if axis == "x":
            return [(row_of(0, x + d, y), col) for d in (1, 2, 3)]
        return [(row_of(0, x, y + d), col) for d in (1, 2, 3)]

    inputs = [(dest_hbm, dest_ref), (rhs_hbm, rhs_ref), (mask_hbm, mask_ref), (diag_hbm, diag_ref)]
    inputs = [pltpu.make_async_copy(src, dst, in_sem.at[i]) for i, (src, dst) in enumerate(inputs)]
    for copy in inputs:
        copy.start()
    near = [(row_of(0, x + a, y), ((z + b) % 4) * 2 + core) for a in range(4) for b in range(4) if a or b]
    near += line("y") + [sibling]
    barrier = pltpu.get_barrier_semaphore()
    for dev in near:
        pl.semaphore_signal(barrier, inc=1, device_id=dev, device_id_type=MESH)

    loads = [pltpu.make_async_copy(w_hbm.at[l, 0, :, :, 0], raw.at[l], load_sem.at[l]) for l in range(3)]
    for load in loads:
        load.start()

    def loads_wait(l):
        pltpu.make_async_copy(w_hbm.at[l, 0, :, :, 0], raw.at[l], load_sem.at[l]).wait()

    out_row, in_row = iota((256, 256), 0), iota((256, 256), 1)
    perm = one_hot(in_row == (out_row & 15) * 16 + (out_row >> 4))

    def relayout(l):
        def one(i, carry):
            zz, cc = i // 2, i % 2
            scale = [mask_ref[l, 0, i, 0, p].astype(F32) for p in range(16)]
            for k0 in range(0, 8, 2):
                piece = jnp.concatenate(
                    [raw[l, i, (k0 + s) * 16:(k0 + s + 1) * 16].reshape(256, B) for s in range(2)], axis=1
                )
                moved = dot(perm, piece)
                for p in range(16):
                    for s in range(2):
                        tile = moved[p * 16:(p + 1) * 16, s * B:(s + 1) * B] * scale[p]
                        wd[l, p, cc, zz, (k0 + s) * 16:(k0 + s + 1) * 16, :] = tile.astype(BF16)
            return carry

        lax.fori_loop(0, 8, one, 0)

    def put_solved(l, residual):
        solved = dot(diag_ref[l], residual).astype(BF16)
        return solved

    def prepare(l, carry):
        loads_wait(l)
        relayout(l)
        return carry

    for copy in inputs[:2]:
        copy.wait()
    dest = dest_ref[...]
    owner = (dest >> 7) & 127
    place = (dest >> 14) * B + (dest & 127)
    owned = one_hot(iota((128, 512), 0) == owner)
    before = dot(owned, one_hot(iota((512, 512), 0) < iota((512, 512), 1)))
    rank = jnp.sum(owned.astype(F32) * before, axis=0, keepdims=True)
    slot = owner * 4 + rank.astype(jnp.int32)
    sort = one_hot(iota((512, 512), 0) == slot)
    rows_out[...] = dot(sort, rhs_ref[...].astype(BF16)).astype(BF16).reshape(64, 8, N)
    lane = iota((128, 512), 0)
    digit = jnp.where(lane < 8, place >> 4, place & 15)
    digit = jnp.where((lane < 16) & ((lane & 7) == (slot & 7)), digit, 0).astype(F32).astype(BF16)
    meta_out[...] = dot_rows(one_hot(iota((64, 512), 0) == (slot >> 3)), digit).reshape(64, 1, B)

    def rows_copy(t, dev):
        return remote(rows_out.at[t], rows_in.at[chip], rows_s, rows_r, dev)

    def meta_copy(t, dev):
        return remote(meta_out.at[t], meta_in.at[chip], meta_s, meta_r, dev)

    pl.semaphore_wait(barrier, len(near))
    for dev in line("y"):
        pl.semaphore_signal(hello, inc=1, device_id=dev, device_id_type=MESH)
    for copy in inputs[2:]:
        copy.wait()
    prepare(0, 0)
    pl.semaphore_wait(hello, 3)

    def send_rows(k, carry):
        t, dev = chip_peer(k)
        meta_copy(t, dev).start()
        rows_copy(t, dev).start()
        return carry

    lax.fori_loop(1, 64, send_rows, 0)
    rows_in[chip] = rows_out[chip]
    meta_in[chip] = meta_out[chip]

    lax.fori_loop(1, 3, prepare, 0)

    some = pl.ds(0, 63)
    all_rows = remote(rows_out.at[some], rows_in.at[some], rows_s, rows_r, sibling)
    all_meta = remote(meta_out.at[some], meta_in.at[some], meta_s, meta_r, sibling)
    all_meta.wait_recv()
    meta_swap = remote(meta_in, meta_sib, mix_s.at[0], mix_r.at[0], sibling)
    meta_swap.start()
    all_rows.wait_recv()
    to, at = iota((512, 512), 0), iota((512, 512), 1)
    half = jnp.where(to < 256, core, other)
    mixed = dot(one_hot(at == (to & 63) * 8 + half * 4 + ((to >> 6) & 3)), rows_in[...].reshape(512, N)).astype(BF16)
    mix_out[...] = mixed[256:]
    mix_swap = remote(mix_out, mix_in, mix_s.at[1], mix_r.at[1], sibling)
    mix_swap.start()

    def place_rows(meta, rows):
        digits = jnp.concatenate([meta.reshape(64, B)] * 4, axis=0)
        at_lane, k = iota((256, B), 1), iota((256, B), 0) >> 6
        mine = (at_lane < 16) & ((at_lane & 7) == core * 4 + k)
        weight = jnp.where(iota((8, B), 1) < 8, 16.0, 1.0).astype(BF16)
        where = dot_rows(weight, jnp.where(mine, digits, 0.0).astype(BF16))[:1]
        return dot(one_hot(iota((512, 256), 0) == where.astype(jnp.int32)), rows)

    total = place_rows(meta_in[...], mixed[:256])
    meta_swap.wait_recv()
    mix_swap.wait_recv()
    ordered_ref[...] = (total + place_rows(meta_sib[...], mix_in[...])).reshape(NLEV, B, N)

    level0 = put_solved(0, ordered_ref[0].astype(BF16))
    gath[0, 0, row] = level0[:, :B]
    gath[0, 1, row] = level0[:, B:]
    solved_t[0] = level0.astype(F32).T

    def gather_copy(l, h, slot, idx, dev):
        return remote(gath.at[l, h, slot], gath.at[l, h, slot], ag_s.at[l, h, idx], ag_r.at[l, h, idx], dev)

    def pair_rhs(l, p):
        return jnp.concatenate([gath[l, 0, p], gath[l, 1, p]], axis=1)

    def down(l, carry):
        for h in range(2):
            u, v = first if h == 0 else second
            for d in (2, 1, 3):
                gather_copy(l, h, row, d - 1, (row_of(h, u + d, v), col)).start()
        for e in (0, 1, 3, 2):
            for h in range(2):
                u, v = first if h == 0 else second
                slot = row_of(h, u - e, v)
                if e:
                    gather_copy(l, h, slot, e - 1, (row, col)).wait_recv()
                for d in (2, 1, 3):
                    gather_copy(l, h, slot, 3 + e * 3 + d - 1, (row_of(h, u, v + d), col)).start()
        order = [(a, b) for a in (0, 1, 3) for b in (0, 1, 3)] + [(a, b) for a in range(4) for b in range(4) if 2 in (a, b)]

        def arrive(a, b):
            for h in range(2):
                e, d = (a, b) if h == 0 else (b, a)
                u, v = first if h == 0 else second
                if d:
                    gather_copy(l, h, row_of(h, u - e, v - d), 3 + e * 3 + d - 1, (row, col)).wait_recv()

        def operands(some):
            slots = [row_of(0, x - a, y - b) for a, b in some]
            rhs = jnp.concatenate([pair_rhs(l, p) for p in slots], axis=0)
            return slots, rhs

        def lhs(slots, c, r, n):
            return jnp.concatenate([wd[l, p, c, r:r + n].reshape(n * B, B) for p in slots], axis=1)

        for a, b in order[:8]:
            arrive(a, b)
        slots, rhs = operands(order[:8])
        for c in range(2):
            for r in range(0, 4, 2):
                acc[c, r:r + 2] = dot(lhs(slots, c, r, 2), rhs).reshape(2, B, N)
        for a, b in order[8:]:
            arrive(a, b)
        slots, rhs = operands(order[8:])
        for step, c in enumerate((other, core)):
            for half in range(2):
                r = ((z // 2 + 1 - half) % 2) * 2
                left = jnp.concatenate([wd[l, p, c, pl.ds(r, 2)].reshape(2 * B, B) for p in slots], axis=1)
                total = acc[c, pl.ds(r, 2)] + dot(left, rhs).reshape(2, B, N)
                if step == 0:
                    sib_out[l, pl.ds(r, 2)] = total.astype(BF16)
                    for s in range(2):
                        remote(sib_out.at[l, r + s], sib_in.at[l, r + s], sib_s.at[l, half * 2 + s], sib_r.at[l, r + s], sibling).start()
                else:
                    acc[c, pl.ds(r, 2)] = total
        for d in (2, 1, 3, 0):
            zz = (z + d) % 4
            remote(sib_out.at[l, zz], sib_in.at[l, zz], sib_s.at[l, 0], sib_r.at[l, zz], sibling).wait_recv()
            total = acc[core, zz] + sib_in[l, zz].astype(F32)
            if d:
                z_out[l, d - 1] = total.astype(BF16)
                remote(z_out.at[l, d - 1], z_in.at[l, d - 1], z_s.at[l, d - 1], z_r.at[l, d - 1], z_peer(d)).start()
            else:
                own = total
        for d in (1, 3, 2):
            remote(z_out.at[l, d - 1], z_in.at[l, d - 1], z_s.at[l, d - 1], z_r.at[l, d - 1], z_peer(d)).wait_recv()
            own = own + z_in[l, d - 1].astype(F32)
        residual = (ordered_ref[l + 1] - own).astype(BF16)
        solved = put_solved(l + 1, residual)
        gath[l + 1, 0, row] = solved[:, :B]
        gath[l + 1, 1, row] = solved[:, B:]
        solved_t[l + 1] = solved.astype(F32).T
        return carry

    lax.fori_loop(0, 3, down, 0)

    def finish(l, slot, residual_t):
        sol_t = dot(residual_t.astype(BF16), diag_ref[l]).astype(BF16)
        upper[slot, core, z] = sol_t
        return sol_t

    def out_copy(l):
        return pltpu.make_async_copy(out_ref.at[l], out_hbm.at[l], out_sem.at[l])

    def emit(l, sol_t):
        out_ref[l] = sol_t.astype(F32).T.astype(BF16)
        out_copy(l).start()

    top = finish(3, 0, solved_t[3])
    emit(3, top)

    def up_copy(t, d):
        return remote(upper.at[t, core, z], upper.at[t, core, z], up_s.at[t, d - 1], up_r.at[t, d - 1], z_peer(d))

    def forward_copy(t, d):
        slot = upper.at[t, core, (z - d) % 4]
        return remote(slot, slot, fw_s.at[t, d], fw_r.at[t, d], sibling)

    def part_copy(t, h, du, dv):
        u, v = first if h == 0 else second
        return remote(
            part_out.at[t, h, du, dv], part_in.at[t, h, du, dv],
            p1_s.at[t, h, du, dv], p1_r.at[t, h, du, dv], (row_of(h, u + du, v), col),
        )

    def line_copy(t, h, dv):
        u, v = first if h == 0 else second
        return remote(
            line_out.at[t, h, dv], line_in.at[t, h, dv], p2_s.at[t, h, dv], p2_r.at[t, h, dv], (row_of(h, u, v + dv), col)
        )

    def up(t, carry):
        l = 2 - t
        for d in (2, 1, 3):
            up_copy(t, d).start()
        forward_copy(t, 0).start()
        for d in (1, 3, 2):
            slot = upper.at[t, core, (z - d) % 4]
            remote(slot, slot, up_s.at[t, d - 1], up_r.at[t, d - 1], sibling).wait_recv()
            forward_copy(t, d).start()
        for d in (0, 1, 3, 2):
            slot = upper.at[t, other, (z - d) % 4]
            remote(slot, slot, fw_s.at[t, d], fw_r.at[t, d], sibling).wait_recv()
        left = jnp.concatenate([upper[t, c, r] for c in range(2) for r in range(4)], axis=1)
        pairs = [((2, 2), (2, 1)), ((2, 3), (1, 2)), ((3, 2), (1, 1)), ((1, 3), (3, 1)),
                 ((3, 3), (0, 2)), ((2, 0), (0, 1)), ((1, 0), (0, 3)), ((3, 0), (0, 0))]
        for two in pairs:
            slots = [row_of(0, x + a, y + b) for a, b in two]
            right = jnp.concatenate([wd[l, p].reshape(8 * B, B) for p in slots], axis=1)
            value = dot(left, right).astype(BF16)
            for s, (a, b) in enumerate(two):
                for h in range(2):
                    du, dv = (a, b) if h == 0 else (b, a)
                    part_out[t, h, du, dv] = value[h * B:(h + 1) * B, s * B:(s + 1) * B]
                    if du:
                        part_copy(t, h, du, dv).start()

        def line_sum(h, dv):
            total = part_out[t, h, 0, dv].astype(F32)
            for du in (1, 3, 2):
                part_copy(t, h, du, dv).wait_recv()
                total = total + part_in[t, h, du, dv].astype(F32)
            return total

        for dv in (2, 1, 3):
            for h in range(2):
                line_out[t, h, dv] = line_sum(h, dv).astype(BF16)
                line_copy(t, h, dv).start()
        keep = []
        for h in range(2):
            keep.append(line_sum(h, 0))
        for h in range(2):
            for dv in (1, 3, 2):
                line_copy(t, h, dv).wait_recv()
                keep[h] = keep[h] + line_in[t, h, dv].astype(F32)
        residual_t = solved_t[l] - jnp.concatenate(keep, axis=0)
        sol_t = finish(l, t + 1, residual_t)
        emit(l, sol_t)
        return carry

    lax.fori_loop(0, 3, up, 0)

    def drain_down(l, carry):
        for h in range(2):
            for idx in range(15):
                gather_copy(l, h, row, idx, (row, col)).wait_send()
        for s in range(4):
            remote(sib_out.at[l, s], sib_in.at[l, s], sib_s.at[l, s], sib_r.at[l, s], sibling).wait_send()
        for d in range(1, 4):
            remote(z_out.at[l, d - 1], z_in.at[l, d - 1], z_s.at[l, d - 1], z_r.at[l, d - 1], z_peer(d)).wait_send()
        return carry

    lax.fori_loop(0, 3, drain_down, 0)

    def drain_up(t, carry):
        for h in range(2):
            for du in range(1, 4):
                for dv in range(4):
                    part_copy(t, h, du, dv).wait_send()
            for dv in range(1, 4):
                line_copy(t, h, dv).wait_send()
        for d in range(4):
            forward_copy(t, d).wait_send()
            if d:
                up_copy(t, d).wait_send()
        return carry

    lax.fori_loop(0, 3, drain_up, 0)
    for l in range(NLEV):
        out_copy(l).wait()
    all_rows.wait_send()
    all_meta.wait_send()
    meta_swap.wait_send()
    mix_swap.wait_send()


def solve(rhs, dest, diag, mask, lower):
    hbm = pl.BlockSpec(memory_space=pltpu.HBM)
    dma = pltpu.SemaphoreType.DMA
    return pl.pallas_call(
        solve_kernel,
        out_shape=jax.ShapeDtypeStruct((NLEV, B, N), BF16),
        in_specs=[hbm] * 5,
        out_specs=pl.BlockSpec(memory_space=pl.ANY),
        scratch_shapes=[
            pltpu.SemaphoreType.REGULAR,
            pltpu.VMEM(rhs.shape, F32),
            pltpu.VMEM(dest.shape, jnp.int32),
            pltpu.VMEM(diag.shape, BF16),
            pltpu.SMEM(mask.shape, jnp.int32),
            pltpu.VMEM((NLEV, B, N), BF16),
            pltpu.VMEM((64, 8, N), BF16),
            pltpu.VMEM((64, 8, N), BF16),
            pltpu.VMEM((64, 1, B), F32),
            pltpu.VMEM((64, 1, B), F32),
            pltpu.VMEM((64, 1, B), F32),
            pltpu.VMEM((256, N), BF16),
            pltpu.VMEM((256, N), BF16),
            pltpu.VMEM((NLEV, B, N), F32),
            pltpu.VMEM((3, 8, B, 16, B), BF16),
            pltpu.VMEM((3, 16, 2, 4, B, B), BF16),
            pltpu.VMEM((4, 2, 16, B, B), BF16),
            pltpu.VMEM((2, 4, B, N), F32),
            pltpu.VMEM((3, 4, B, N), BF16),
            pltpu.VMEM((3, 4, B, N), BF16),
            pltpu.VMEM((3, 3, B, N), BF16),
            pltpu.VMEM((3, 3, B, N), BF16),
            pltpu.VMEM((4, N, B), F32),
            pltpu.VMEM((4, 2, 4, N, B), BF16),
            pltpu.VMEM((3, 2, 4, 4, B, B), BF16),
            pltpu.VMEM((3, 2, 4, 4, B, B), BF16),
            pltpu.VMEM((3, 2, 4, B, B), BF16),
            pltpu.VMEM((3, 2, 4, B, B), BF16),
            dma, dma, dma, dma, dma((2,)), dma((2,)),
            dma((4,)), dma((3,)), dma((NLEV,)), dma((3, 2, 15)), dma((3, 2, 15)), dma((3, 4)), dma((3, 4)), dma((3, 3)), dma((3, 3)),
            dma((3, 3)), dma((3, 3)), dma((3, 4)), dma((3, 4)),
            dma((3, 2, 4, 4)), dma((3, 2, 4, 4)), dma((3, 2, 4)), dma((3, 2, 4)),
        ],
        compiler_params=pltpu.CompilerParams(
            collective_id=0, has_side_effects=True, vmem_limit_bytes=50 * 1024 * 1024
        ),
    )(*[pltpu.with_memory_space_constraint(a, pltpu.HBM) for a in (rhs, dest, diag, mask, lower)])


def per_device(rhs_rows, dest_row, diag_inverse, lower_blocks, block_mask):
    dest = dest_row.reshape(1, dest_row.shape[0])
    return solve(rhs_rows, dest, diag_inverse[:, 0], block_mask, lower_blocks)[:, None]


def solution(mesh):
    in_specs = (
        P(("row", "col"), None),
        P(("row", "col")),
        P(None, ("row", "col"), None, None),
        P(None, "row", None, None, "col", None, None),
        P(None, "row", None, "col", None),
    )
    out_specs = P(None, ("row", "col"), None, None)
    return jax.shard_map(per_device, mesh=mesh, in_specs=in_specs, out_specs=out_specs, check_vma=False)
```

```python
import jax
import jax.numpy as jnp
from jax import lax
from jax.experimental import pallas as pl
from jax.experimental.pallas import tpu as pltpu
from jax.sharding import PartitionSpec as P

B = 128
NLEV = 4
N = 256
C = 128
H = 64
MESH = pl.DeviceIdType.MESH
F32 = jnp.float32
BF16 = jnp.bfloat16


def dot(a, b):
    return jnp.dot(a, b, preferred_element_type=F32)


def dot_rows(a, b):
    return lax.dot_general(a, b, (((1,), (1,)), ((), ())), preferred_element_type=F32)


def one_hot(condition):
    return jnp.where(condition, 1.0, 0.0).astype(BF16)


def iota(shape, axis):
    return lax.broadcasted_iota(jnp.int32, shape, axis)


def solve_kernel(
    rhs_hbm, dest_hbm, diag_hbm, mask_hbm, w_hbm, out_hbm,
    hello, rhs_ref, dest_ref, diag_ref, mask_ref, out_ref,     rows_out, rows_in, meta_out, meta_in, meta_sib, mix_out, mix_in, ordered_ref, raw, wd, gath, acc, sib_out, sib_in, z_out, z_in, solved_t, upper, part_out, part_in, line_out, line_in,
    rows_s, rows_r, meta_s, meta_r, mix_s, mix_r, in_sem, load_sem, out_sem, ag_s, ag_r, sib_s, sib_r, z_s, z_r, up_s, up_r, fw_s, fw_r, p1_s, p1_r, p2_s, p2_r,
):
    row = lax.axis_index("row")
    col = lax.axis_index("col")
    x, y = row // 4, row % 4
    z, core = col // 2, col % 2
    other = 1 - core

    def row_of(h, u, v):
        return (u % 4) * 4 + v % 4 if h == 0 else (v % 4) * 4 + u % 4

    def remote(src, dst, ssem, rsem, dev):
        return pltpu.make_async_remote_copy(
            src_ref=src, dst_ref=dst, send_sem=ssem, recv_sem=rsem, device_id=dev, device_id_type=MESH
        )

    sibling = (row, z * 2 + other)

    def z_peer(d):
        return (row, ((z + d) % 4) * 2 + core)

    chip = row * 4 + z

    def chip_peer(k):
        t = (chip + k) % 64
        return t, (t // 4, (t % 4) * 2 + core)

    def line(axis):
        if axis == "x":
            return [(row_of(0, x + d, y), col) for d in (1, 2, 3)]
        return [(row_of(0, x, y + d), col) for d in (1, 2, 3)]

    inputs = [(dest_hbm, dest_ref), (rhs_hbm, rhs_ref), (mask_hbm, mask_ref), (diag_hbm, diag_ref)]
    inputs = [pltpu.make_async_copy(src, dst, in_sem.at[i]) for i, (src, dst) in enumerate(inputs)]
    for copy in inputs:
        copy.start()
    near = [(row_of(0, x + a, y), ((z + b) % 4) * 2 + core) for a in range(4) for b in range(4) if a or b]
    near += line("y") + [sibling]
    barrier = pltpu.get_barrier_semaphore()
    for dev in near:
        pl.semaphore_signal(barrier, inc=1, device_id=dev, device_id_type=MESH)

    loads = [pltpu.make_async_copy(w_hbm.at[l, 0, :, :, 0], raw.at[l], load_sem.at[l]) for l in range(3)]
    for load in loads:
        load.start()

    def loads_wait(l):
        pltpu.make_async_copy(w_hbm.at[l, 0, :, :, 0], raw.at[l], load_sem.at[l]).wait()

    out_row, in_row = iota((256, 256), 0), iota((256, 256), 1)
    perm = one_hot(in_row == (out_row & 15) * 16 + (out_row >> 4))

    def relayout(l):
        def one(i, carry):
            zz, cc = i // 2, i % 2
            scale = [mask_ref[l, 0, i, 0, p].astype(F32) for p in range(16)]
            for k0 in range(0, 8, 2):
                piece = jnp.concatenate(
                    [raw[l, i, (k0 + s) * 16:(k0 + s + 1) * 16].reshape(256, B) for s in range(2)], axis=1
                )
                moved = dot(perm, piece)
                for p in range(16):
                    for s in range(2):
                        tile = moved[p * 16:(p + 1) * 16, s * B:(s + 1) * B] * scale[p]
                        wd[l, p, cc, zz, (k0 + s) * 16:(k0 + s + 1) * 16, :] = tile.astype(BF16)
            return carry

        lax.fori_loop(0, 8, one, 0)

    def prepare(l, carry):
        loads_wait(l)
        relayout(l)
        return carry

    for copy in inputs[:2]:
        copy.wait()
    dest = dest_ref[...]
    owner = (dest >> 7) & 127
    place = (dest >> 14) * B + (dest & 127)
    owned = one_hot(iota((128, 512), 0) == owner)
    before = dot(owned, one_hot(iota((512, 512), 0) < iota((512, 512), 1)))
    rank = jnp.sum(owned.astype(F32) * before, axis=0, keepdims=True)
    slot = owner * 4 + rank.astype(jnp.int32)
    sort = one_hot(iota((512, 512), 0) == slot)
    rows_out[...] = dot(sort, rhs_ref[...].astype(BF16)).astype(BF16).reshape(64, 8, N)
    lane = iota((128, 512), 0)
    digit = jnp.where(lane < 8, place >> 4, place & 15)
    digit = jnp.where((lane < 16) & ((lane & 7) == (slot & 7)), digit, 0).astype(F32).astype(BF16)
    meta_out[...] = dot_rows(one_hot(iota((64, 512), 0) == (slot >> 3)), digit).reshape(64, 1, B)

    def rows_copy(t, dev):
        return remote(rows_out.at[t], rows_in.at[chip], rows_s, rows_r, dev)

    def meta_copy(t, dev):
        return remote(meta_out.at[t], meta_in.at[chip], meta_s, meta_r, dev)

    pl.semaphore_wait(barrier, len(near))
    for dev in line("y"):
        pl.semaphore_signal(hello, inc=1, device_id=dev, device_id_type=MESH)
    for copy in inputs[2:]:
        copy.wait()
    prepare(0, 0)
    pl.semaphore_wait(hello, 3)

    def send_rows(k, carry):
        t, dev = chip_peer(k)
        meta_copy(t, dev).start()
        rows_copy(t, dev).start()
        return carry

    lax.fori_loop(1, 64, send_rows, 0)
    rows_in[chip] = rows_out[chip]
    meta_in[chip] = meta_out[chip]

    lax.fori_loop(1, 3, prepare, 0)

    some = pl.ds(0, 63)
    all_rows = remote(rows_out.at[some], rows_in.at[some], rows_s, rows_r, sibling)
    all_meta = remote(meta_out.at[some], meta_in.at[some], meta_s, meta_r, sibling)
    all_meta.wait_recv()
    meta_swap = remote(meta_in, meta_sib, mix_s.at[0], mix_r.at[0], sibling)
    meta_swap.start()
    all_rows.wait_recv()
    to, at = iota((512, 512), 0), iota((512, 512), 1)
    half = jnp.where(to < 256, core, other)
    mixed = dot(one_hot(at == (to & 63) * 8 + half * 4 + ((to >> 6) & 3)), rows_in[...].reshape(512, N)).astype(BF16)
    mix_out[...] = mixed[256:]
    mix_swap = remote(mix_out, mix_in, mix_s.at[1], mix_r.at[1], sibling)
    mix_swap.start()

    def place_rows(meta, rows):
        digits = jnp.concatenate([meta.reshape(64, B)] * 4, axis=0)
        at_lane, k = iota((256, B), 1), iota((256, B), 0) >> 6
        mine = (at_lane < 16) & ((at_lane & 7) == core * 4 + k)
        weight = jnp.where(iota((8, B), 1) < 8, 16.0, 1.0).astype(BF16)
        where = dot_rows(weight, jnp.where(mine, digits, 0.0).astype(BF16))[:1]
        return dot(one_hot(iota((512, 256), 0) == where.astype(jnp.int32)), rows)

    total = place_rows(meta_in[...], mixed[:256])
    meta_swap.wait_recv()
    mix_swap.wait_recv()
    ordered_ref[...] = (total + place_rows(meta_sib[...], mix_in[...])).reshape(NLEV, B, N)

    def set_solved(l, s, residual):
        solved = dot(diag_ref[l], residual).astype(BF16)
        gath[l, s, row] = solved
        solved_t[l, s] = solved.astype(F32).T

    def axes(h):
        return (x, y) if h == 0 else (y, x)

    def gather_copy(l, s, h, slot, idx, dev):
        rows = gath.at[l, s, slot, pl.ds(h * H, H)]
        return remote(rows, rows, ag_s.at[l, s, h, idx], ag_r.at[l, s, h, idx], dev)

    def relay(l, s, h, e):
        u, v = axes(h)
        slot = row_of(h, u - e, v)
        if e:
            gather_copy(l, s, h, slot, e - 1, (row, col)).wait_recv()
        for d in (2, 1, 3):
            gather_copy(l, s, h, slot, 3 + e * 3 + d - 1, (row_of(h, u, v + d), col)).start()

    def down_send(l, s):
        for h in range(2):
            u, v = axes(h)
            for d in (2, 1, 3):
                gather_copy(l, s, h, row, d - 1, (row_of(h, u + d, v), col)).start()
        for h in range(2):
            relay(l, s, h, 0)

    def down_relay(l, s):
        for e in (1, 3, 2):
            for h in range(2):
                relay(l, s, h, e)

    order = [(a, b) for a in (0, 1, 3) for b in (0, 1, 3)] + [(a, b) for a in range(4) for b in range(4) if 2 in (a, b)]

    def operands(l, s, some):
        slots = [row_of(0, x - a, y - b) for a, b in some]
        for a, b in some:
            for h in range(2):
                e, d = (a, b) if h == 0 else (b, a)
                u, v = axes(h)
                if d:
                    gather_copy(l, s, h, row_of(h, u - e, v - d), 3 + e * 3 + d - 1, (row, col)).wait_recv()
        return slots, jnp.concatenate([gath[l, s, p] for p in slots], axis=0)

    def down_first(l, s):
        slots, rhs = operands(l, s, order[:8])
        for c in range(2):
            for r in range(0, 4, 2):
                left = jnp.concatenate([wd[l, p, c, r:r + 2].reshape(2 * B, B) for p in slots], axis=1)
                acc[s, c, r:r + 2] = dot(left, rhs).reshape(2, B, C)

    def sib_copy(l, s, zz, send):
        return remote(sib_out.at[l, s, zz], sib_in.at[l, s, zz], sib_s.at[l, s, send], sib_r.at[l, s, zz], sibling)

    def z_copy(l, s, d):
        return remote(z_out.at[l, s, d - 1], z_in.at[l, s, d - 1], z_s.at[l, s, d - 1], z_r.at[l, s, d - 1], z_peer(d))

    def down_second(l, s):
        slots, rhs = operands(l, s, order[8:])
        for step, c in enumerate((other, core)):
            for half in range(2):
                r = ((z // 2 + 1 - half) % 2) * 2
                left = jnp.concatenate([wd[l, p, c, pl.ds(r, 2)].reshape(2 * B, B) for p in slots], axis=1)
                total = acc[s, c, pl.ds(r, 2)] + dot(left, rhs).reshape(2, B, C)
                if step == 0:
                    sib_out[l, s, pl.ds(r, 2)] = total.astype(BF16)
                    for k in range(2):
                        sib_copy(l, s, r + k, half * 2 + k).start()
                else:
                    acc[s, c, pl.ds(r, 2)] = total

    def chip_sum(l, s, d):
        zz = (z + d) % 4
        sib_copy(l, s, zz, 0).wait_recv()
        return acc[s, core, zz] + sib_in[l, s, zz].astype(F32)

    def down_line(l, s):
        for d in (2, 1, 3):
            z_out[l, s, d - 1] = chip_sum(l, s, d).astype(BF16)
            z_copy(l, s, d).start()

    def down_finish(l, s):
        own = ordered_ref[l + 1, :, s * C:(s + 1) * C] - chip_sum(l, s, 0)
        for d in (1, 3, 2):
            z_copy(l, s, d).wait_recv()
            own = own - z_in[l, s, d - 1].astype(F32)
        set_solved(l + 1, s, own.astype(BF16))

    def out_copy(l):
        return pltpu.make_async_copy(out_ref.at[l], out_hbm.at[l], out_sem.at[l])

    def finish(l, slot, s, residual_t):
        sol_t = dot(residual_t.astype(BF16), diag_ref[l]).astype(BF16)
        upper[slot, s, core, z] = sol_t
        return sol_t

    def emit(l, s, sol_t):
        out_ref[l, :, s * C:(s + 1) * C] = sol_t.astype(F32).T.astype(BF16)
        if s == 1:
            out_copy(l).start()

    def up_copy(t, s, d):
        slot = upper.at[t, s, core, z]
        return remote(slot, slot, up_s.at[t, s, d - 1], up_r.at[t, s, d - 1], z_peer(d))

    def forward_copy(t, s, d):
        slot = upper.at[t, s, core, (z - d) % 4]
        return remote(slot, slot, fw_s.at[t, s, d], fw_r.at[t, s, d], sibling)

    def part_copy(t, s, h, du, dv):
        u, v = axes(h)
        return remote(
            part_out.at[t, s, h, du, dv], part_in.at[t, s, h, du, dv],
            p1_s.at[t, s, h, du, dv], p1_r.at[t, s, h, du, dv], (row_of(h, u + du, v), col),
        )

    def line_copy(t, s, h, dv):
        u, v = axes(h)
        return remote(
            line_out.at[t, s, h, dv], line_in.at[t, s, h, dv],
            p2_s.at[t, s, h, dv], p2_r.at[t, s, h, dv], (row_of(h, u, v + dv), col),
        )

    def up_send(t, s):
        for d in (2, 1, 3):
            up_copy(t, s, d).start()
        forward_copy(t, s, 0).start()

    def up_forward(t, s):
        for d in (1, 3, 2):
            slot = upper.at[t, s, core, (z - d) % 4]
            remote(slot, slot, up_s.at[t, s, d - 1], up_r.at[t, s, d - 1], sibling).wait_recv()
            forward_copy(t, s, d).start()

    def up_parts(t, s):
        for d in (0, 1, 3, 2):
            slot = upper.at[t, s, other, (z - d) % 4]
            remote(slot, slot, fw_s.at[t, s, d], fw_r.at[t, s, d], sibling).wait_recv()
        left = jnp.concatenate([upper[t, s, c, r] for c in range(2) for r in range(4)], axis=1)
        pairs = [((2, 2), (2, 1)), ((2, 3), (1, 2)), ((3, 2), (1, 1)), ((1, 3), (3, 1)),
                 ((3, 3), (0, 2)), ((2, 0), (0, 1)), ((1, 0), (0, 3)), ((3, 0), (0, 0))]
        for two in pairs:
            slots = [row_of(0, x + a, y + b) for a, b in two]
            right = jnp.concatenate([wd[2 - t, p].reshape(8 * B, B) for p in slots], axis=1)
            value = dot(left, right).astype(BF16)
            for k, (a, b) in enumerate(two):
                for h in range(2):
                    du, dv = (a, b) if h == 0 else (b, a)
                    part_out[t, s, h, du, dv] = value[h * H:(h + 1) * H, k * B:(k + 1) * B]
                    if du:
                        part_copy(t, s, h, du, dv).start()

    def line_sum(t, s, h, dv):
        total = part_out[t, s, h, 0, dv].astype(F32)
        for du in (1, 3, 2):
            part_copy(t, s, h, du, dv).wait_recv()
            total = total + part_in[t, s, h, du, dv].astype(F32)
        return total

    def up_lines(t, s):
        for dv in (2, 1, 3):
            for h in range(2):
                line_out[t, s, h, dv] = line_sum(t, s, h, dv).astype(BF16)
                line_copy(t, s, h, dv).start()

    def up_finish(t, s):
        keep = []
        for h in range(2):
            total = line_sum(t, s, h, 0)
            for dv in (1, 3, 2):
                line_copy(t, s, h, dv).wait_recv()
                total = total + line_in[t, s, h, dv].astype(F32)
            keep.append(total)
        residual_t = solved_t[2 - t, s] - jnp.concatenate(keep, axis=0)
        emit(2 - t, s, finish(2 - t, t + 1, s, residual_t))

    def top(s):
        emit(3, s, finish(3, 0, s, solved_t[3, s]))

    for s in range(2):
        set_solved(0, s, ordered_ref[0, :, s * C:(s + 1) * C].astype(BF16))

    def down(l, carry):
        down_send(l, 0)

        @pl.when(l > 0)
        def _():
            down_first(l - 1, 1)
            down_second(l - 1, 1)
            down_line(l - 1, 1)

        down_relay(l, 0)

        @pl.when(l > 0)
        def _():
            down_finish(l - 1, 1)

        down_send(l, 1)
        down_first(l, 0)
        down_second(l, 0)
        down_line(l, 0)
        down_relay(l, 1)
        down_finish(l, 0)
        return carry

    lax.fori_loop(0, 3, down, 0)
    top(0)

    def up(t, carry):
        up_send(t, 0)

        @pl.when(t == 0)
        def _():
            down_first(2, 1)
            down_second(2, 1)
            down_line(2, 1)

        @pl.when(t > 0)
        def _():
            up_lines(t - 1, 1)

        up_forward(t, 0)
        up_parts(t, 0)

        @pl.when(t == 0)
        def _():
            down_finish(2, 1)
            top(1)

        @pl.when(t > 0)
        def _():
            up_finish(t - 1, 1)

        up_send(t, 1)
        up_lines(t, 0)
        up_forward(t, 1)
        up_parts(t, 1)
        up_finish(t, 0)
        return carry

    lax.fori_loop(0, 3, up, 0)
    up_lines(2, 1)
    up_finish(2, 1)

    def drain_down(l, carry):
        for s in range(2):
            for h in range(2):
                for idx in range(15):
                    gather_copy(l, s, h, row, idx, (row, col)).wait_send()
            for k in range(4):
                sib_copy(l, s, k, k).wait_send()
            for d in range(1, 4):
                z_copy(l, s, d).wait_send()
        return carry

    lax.fori_loop(0, 3, drain_down, 0)

    def drain_up(t, carry):
        for s in range(2):
            for h in range(2):
                for du in range(1, 4):
                    for dv in range(4):
                        part_copy(t, s, h, du, dv).wait_send()
                for dv in range(1, 4):
                    line_copy(t, s, h, dv).wait_send()
            for d in range(4):
                forward_copy(t, s, d).wait_send()
                if d:
                    up_copy(t, s, d).wait_send()
        return carry

    lax.fori_loop(0, 3, drain_up, 0)
    for l in range(NLEV):
        out_copy(l).wait()
    all_rows.wait_send()
    all_meta.wait_send()
    meta_swap.wait_send()
    mix_swap.wait_send()


def solve(rhs, dest, diag, mask, lower):
    hbm = pl.BlockSpec(memory_space=pltpu.HBM)
    dma = pltpu.SemaphoreType.DMA
    return pl.pallas_call(
        solve_kernel,
        out_shape=jax.ShapeDtypeStruct((NLEV, B, N), BF16),
        in_specs=[hbm] * 5,
        out_specs=pl.BlockSpec(memory_space=pl.ANY),
        scratch_shapes=[
            pltpu.SemaphoreType.REGULAR,
            pltpu.VMEM(rhs.shape, F32),
            pltpu.VMEM(dest.shape, jnp.int32),
            pltpu.VMEM(diag.shape, BF16),
            pltpu.SMEM(mask.shape, jnp.int32),
            pltpu.VMEM((NLEV, B, N), BF16),
            pltpu.VMEM((64, 8, N), BF16),
            pltpu.VMEM((64, 8, N), BF16),
            pltpu.VMEM((64, 1, B), F32),
            pltpu.VMEM((64, 1, B), F32),
            pltpu.VMEM((64, 1, B), F32),
            pltpu.VMEM((256, N), BF16),
            pltpu.VMEM((256, N), BF16),
            pltpu.VMEM((NLEV, B, N), F32),
            pltpu.VMEM((3, 8, B, 16, B), BF16),
            pltpu.VMEM((3, 16, 2, 4, B, B), BF16),
            pltpu.VMEM((4, 2, 16, B, C), BF16),
            pltpu.VMEM((2, 2, 4, B, C), F32),
            pltpu.VMEM((3, 2, 4, B, C), BF16),
            pltpu.VMEM((3, 2, 4, B, C), BF16),
            pltpu.VMEM((3, 2, 3, B, C), BF16),
            pltpu.VMEM((3, 2, 3, B, C), BF16),
            pltpu.VMEM((4, 2, C, B), F32),
            pltpu.VMEM((4, 2, 2, 4, C, B), BF16),
            pltpu.VMEM((3, 2, 2, 4, 4, H, B), BF16),
            pltpu.VMEM((3, 2, 2, 4, 4, H, B), BF16),
            pltpu.VMEM((3, 2, 2, 4, H, B), BF16),
            pltpu.VMEM((3, 2, 2, 4, H, B), BF16),
            dma, dma, dma, dma, dma((2,)), dma((2,)),
            dma((4,)), dma((3,)), dma((NLEV,)), dma((3, 2, 2, 15)), dma((3, 2, 2, 15)), dma((3, 2, 4)), dma((3, 2, 4)),
            dma((3, 2, 3)), dma((3, 2, 3)), dma((3, 2, 3)), dma((3, 2, 3)), dma((3, 2, 4)), dma((3, 2, 4)),
            dma((3, 2, 2, 4, 4)), dma((3, 2, 2, 4, 4)), dma((3, 2, 2, 4)), dma((3, 2, 2, 4)),
        ],
        compiler_params=pltpu.CompilerParams(
            collective_id=0, has_side_effects=True, vmem_limit_bytes=50 * 1024 * 1024
        ),
    )(*[pltpu.with_memory_space_constraint(a, pltpu.HBM) for a in (rhs, dest, diag, mask, lower)])


def per_device(rhs_rows, dest_row, diag_inverse, lower_blocks, block_mask):
    dest = dest_row.reshape(1, dest_row.shape[0])
    return solve(rhs_rows, dest, diag_inverse[:, 0], block_mask, lower_blocks)[:, None]


def solution(mesh):
    in_specs = (
        P(("row", "col"), None),
        P(("row", "col")),
        P(None, ("row", "col"), None, None),
        P(None, "row", None, None, "col", None, None),
        P(None, "row", None, "col", None),
    )
    out_specs = P(None, ("row", "col"), None, None)
    return jax.shard_map(per_device, mesh=mesh, in_specs=in_specs, out_specs=out_specs, check_vma=False)
```

```python
import jax
import jax.numpy as jnp
from jax import lax
from jax.experimental import pallas as pl
from jax.experimental.pallas import tpu as pltpu
from jax.sharding import PartitionSpec as P

B = 128
NLEV = 4
N = 256
C = 128
H = 64
MESH = pl.DeviceIdType.MESH
F32 = jnp.float32
BF16 = jnp.bfloat16


def dot(a, b):
    return jnp.dot(a, b, preferred_element_type=F32)


def dot_rows(a, b):
    return lax.dot_general(a, b, (((1,), (1,)), ((), ())), preferred_element_type=F32)


def one_hot(condition):
    return jnp.where(condition, 1.0, 0.0).astype(BF16)


def iota(shape, axis):
    return lax.broadcasted_iota(jnp.int32, shape, axis)


def solve_kernel(
    rhs_hbm, dest_hbm, diag_hbm, mask_hbm, w_hbm, out_hbm,
    hello, rhs_ref, dest_ref, diag_ref, mask_ref, out_ref,     rows_out, rows_in, meta_out, meta_in, meta_sib, mix_out, mix_in, ordered_ref, raw, wd, gath, acc, col_out, col_in, solved_t, upper, part_out, part_in, line_out, line_in,
    rows_s, rows_r, meta_s, meta_r, mix_s, mix_r, in_sem, load_sem, out_sem, ag_s, ag_r, col_s, col_r, up_s, up_r, fw_s, fw_r, p1_s, p1_r, p2_s, p2_r,
):
    row = lax.axis_index("row")
    col = lax.axis_index("col")
    x, y = row // 4, row % 4
    z, core = col // 2, col % 2
    other = 1 - core

    def row_of(h, u, v):
        return (u % 4) * 4 + v % 4 if h == 0 else (v % 4) * 4 + u % 4

    def remote(src, dst, ssem, rsem, dev):
        return pltpu.make_async_remote_copy(
            src_ref=src, dst_ref=dst, send_sem=ssem, recv_sem=rsem, device_id=dev, device_id_type=MESH
        )

    sibling = (row, z * 2 + other)

    def z_peer(d):
        return (row, ((z + d) % 4) * 2 + core)

    chip = row * 4 + z

    def chip_peer(k):
        t = (chip + k) % 64
        return t, (t // 4, (t % 4) * 2 + core)

    def line(axis):
        if axis == "x":
            return [(row_of(0, x + d, y), col) for d in (1, 2, 3)]
        return [(row_of(0, x, y + d), col) for d in (1, 2, 3)]

    inputs = [(dest_hbm, dest_ref), (rhs_hbm, rhs_ref), (mask_hbm, mask_ref), (diag_hbm, diag_ref)]
    inputs = [pltpu.make_async_copy(src, dst, in_sem.at[i]) for i, (src, dst) in enumerate(inputs)]
    for copy in inputs:
        copy.start()
    near = [(row_of(0, x + a, y), ((z + b) % 4) * 2 + core) for a in range(4) for b in range(4) if a or b]
    near += line("y") + [sibling]
    barrier = pltpu.get_barrier_semaphore()
    for dev in near:
        pl.semaphore_signal(barrier, inc=1, device_id=dev, device_id_type=MESH)

    loads = [pltpu.make_async_copy(w_hbm.at[l, 0, :, :, 0], raw.at[l], load_sem.at[l]) for l in range(3)]
    for load in loads:
        load.start()

    def loads_wait(l):
        pltpu.make_async_copy(w_hbm.at[l, 0, :, :, 0], raw.at[l], load_sem.at[l]).wait()

    out_row, in_row = iota((256, 256), 0), iota((256, 256), 1)
    perm = one_hot(in_row == (out_row & 15) * 16 + (out_row >> 4))

    def relayout(l):
        def one(i, carry):
            zz, cc = i // 2, i % 2
            scale = [mask_ref[l, 0, i, 0, p].astype(F32) for p in range(16)]
            for k0 in range(0, 8, 2):
                piece = jnp.concatenate(
                    [raw[l, i, (k0 + s) * 16:(k0 + s + 1) * 16].reshape(256, B) for s in range(2)], axis=1
                )
                moved = dot(perm, piece)
                for p in range(16):
                    for s in range(2):
                        tile = moved[p * 16:(p + 1) * 16, s * B:(s + 1) * B] * scale[p]
                        wd[l, p, cc, zz, (k0 + s) * 16:(k0 + s + 1) * 16, :] = tile.astype(BF16)
            return carry

        lax.fori_loop(0, 8, one, 0)

    def prepare(l, carry):
        loads_wait(l)
        relayout(l)
        return carry

    for copy in inputs[:2]:
        copy.wait()
    dest = dest_ref[...]
    owner = (dest >> 7) & 127
    place = (dest >> 14) * B + (dest & 127)
    owned = one_hot(iota((128, 512), 0) == owner)
    before = dot(owned, one_hot(iota((512, 512), 0) < iota((512, 512), 1)))
    rank = jnp.sum(owned.astype(F32) * before, axis=0, keepdims=True)
    slot = owner * 4 + rank.astype(jnp.int32)
    sort = one_hot(iota((512, 512), 0) == slot)
    rows_out[...] = dot(sort, rhs_ref[...].astype(BF16)).astype(BF16).reshape(64, 8, N)
    lane = iota((128, 512), 0)
    digit = jnp.where(lane < 8, place >> 4, place & 15)
    digit = jnp.where((lane < 16) & ((lane & 7) == (slot & 7)), digit, 0).astype(F32).astype(BF16)
    meta_out[...] = dot_rows(one_hot(iota((64, 512), 0) == (slot >> 3)), digit).reshape(64, 1, B)

    def rows_copy(t, dev):
        return remote(rows_out.at[t], rows_in.at[chip], rows_s, rows_r, dev)

    def meta_copy(t, dev):
        return remote(meta_out.at[t], meta_in.at[chip], meta_s, meta_r, dev)

    pl.semaphore_wait(barrier, len(near))
    for dev in line("y"):
        pl.semaphore_signal(hello, inc=1, device_id=dev, device_id_type=MESH)
    for copy in inputs[2:]:
        copy.wait()
    prepare(0, 0)
    pl.semaphore_wait(hello, 3)

    def send_rows(k, carry):
        t, dev = chip_peer(k)
        meta_copy(t, dev).start()
        rows_copy(t, dev).start()
        return carry

    lax.fori_loop(1, 64, send_rows, 0)
    rows_in[chip] = rows_out[chip]
    meta_in[chip] = meta_out[chip]

    lax.fori_loop(1, 3, prepare, 0)

    some = pl.ds(0, 63)
    all_rows = remote(rows_out.at[some], rows_in.at[some], rows_s, rows_r, sibling)
    all_meta = remote(meta_out.at[some], meta_in.at[some], meta_s, meta_r, sibling)
    all_meta.wait_recv()
    meta_swap = remote(meta_in, meta_sib, mix_s.at[0], mix_r.at[0], sibling)
    meta_swap.start()
    all_rows.wait_recv()
    to, at = iota((512, 512), 0), iota((512, 512), 1)
    half = jnp.where(to < 256, core, other)
    mixed = dot(one_hot(at == (to & 63) * 8 + half * 4 + ((to >> 6) & 3)), rows_in[...].reshape(512, N)).astype(BF16)
    mix_out[...] = mixed[256:]
    mix_swap = remote(mix_out, mix_in, mix_s.at[1], mix_r.at[1], sibling)
    mix_swap.start()

    def place_rows(meta, rows):
        digits = jnp.concatenate([meta.reshape(64, B)] * 4, axis=0)
        at_lane, k = iota((256, B), 1), iota((256, B), 0) >> 6
        mine = (at_lane < 16) & ((at_lane & 7) == core * 4 + k)
        weight = jnp.where(iota((8, B), 1) < 8, 16.0, 1.0).astype(BF16)
        where = dot_rows(weight, jnp.where(mine, digits, 0.0).astype(BF16))[:1]
        return dot(one_hot(iota((512, 256), 0) == where.astype(jnp.int32)), rows)

    total = place_rows(meta_in[...], mixed[:256])
    meta_swap.wait_recv()
    mix_swap.wait_recv()
    ordered_ref[...] = (total + place_rows(meta_sib[...], mix_in[...])).reshape(NLEV, B, N)

    def set_solved(l, s, residual):
        solved = dot(diag_ref[l], residual).astype(BF16)
        gath[l, s, row] = solved
        solved_t[l, s] = solved.astype(F32).T

    def axes(h):
        return (x, y) if h == 0 else (y, x)

    def gather_copy(l, s, h, slot, idx, dev):
        rows = gath.at[l, s, slot, pl.ds(h * H, H)]
        return remote(rows, rows, ag_s.at[l, s], ag_r.at[l, s, h, idx], dev)

    def relay(l, s, h, e):
        u, v = axes(h)
        slot = row_of(h, u - e, v)
        if e:
            gather_copy(l, s, h, slot, e - 1, (row, col)).wait_recv()
        for d in (2, 1, 3):
            gather_copy(l, s, h, slot, 3 + e * 3 + d - 1, (row_of(h, u, v + d), col)).start()

    def down_send(l, s):
        for h in range(2):
            u, v = axes(h)
            for d in (2, 1, 3):
                gather_copy(l, s, h, row, d - 1, (row_of(h, u + d, v), col)).start()
        for h in range(2):
            relay(l, s, h, 0)

    def down_relay(l, s):
        for e in (1, 3, 2):
            for h in range(2):
                relay(l, s, h, e)

    order = [(a, b) for a in (0, 1, 3) for b in (0, 1, 3)] + [(a, b) for a in range(4) for b in range(4) if 2 in (a, b)]

    def operands(l, s, some):
        slots = [row_of(0, x - a, y - b) for a, b in some]
        for a, b in some:
            for h in range(2):
                e, d = (a, b) if h == 0 else (b, a)
                u, v = axes(h)
                if d:
                    gather_copy(l, s, h, row_of(h, u - e, v - d), 3 + e * 3 + d - 1, (row, col)).wait_recv()
        return slots, jnp.concatenate([gath[l, s, p] for p in slots], axis=0)

    def down_first(l, s):
        slots, rhs = operands(l, s, order[:8])
        for c in range(2):
            for r in range(0, 4, 2):
                left = jnp.concatenate([wd[l, p, c, r:r + 2].reshape(2 * B, B) for p in slots], axis=1)
                acc[s, c, r:r + 2] = dot(left, rhs).reshape(2, B, C)

    def col_copy(l, s, dc, zz):
        d = (zz - z + 4) % 4
        return remote(
            col_out.at[l, s, dc, zz], col_in.at[l, s, dc, d], col_s.at[l, s], col_r.at[l, s, dc, d],
            (row, zz * 2 + (other if dc else core)),
        )

    def down_second(l, s):
        slots, rhs = operands(l, s, order[8:])
        for half in range(2):
            r = ((z // 2 + 1 - half) % 2) * 2
            for dc, c in ((1, other), (0, core)):
                left = jnp.concatenate([wd[l, p, c, pl.ds(r, 2)].reshape(2 * B, B) for p in slots], axis=1)
                total = acc[s, c, pl.ds(r, 2)] + dot(left, rhs).reshape(2, B, C)
                col_out[l, s, dc, pl.ds(r, 2)] = total.astype(BF16)
                if half == 0 or dc == 1:
                    col_copy(l, s, dc, r + z % 2).start()
                else:
                    acc[s, c, pl.ds(r, 2)] = total
                col_copy(l, s, dc, r + 1 - z % 2).start()

    def down_finish(l, s):
        own = ordered_ref[l + 1, :, s * C:(s + 1) * C] - acc[s, core, z]
        for dc, d in ((1, 0), (0, 1), (0, 3), (0, 2), (1, 1), (1, 3), (1, 2)):
            remote(col_out.at[l, s, dc, 0], col_in.at[l, s, dc, d], col_s.at[l, s], col_r.at[l, s, dc, d], sibling).wait_recv()
            own = own - col_in[l, s, dc, d].astype(F32)
        set_solved(l + 1, s, own.astype(BF16))

    def out_copy(l):
        return pltpu.make_async_copy(out_ref.at[l], out_hbm.at[l], out_sem.at[l])

    def finish(l, slot, s, residual_t):
        sol_t = dot(residual_t.astype(BF16), diag_ref[l]).astype(BF16)
        upper[slot, s, core, z] = sol_t
        return sol_t

    def emit(l, s, sol_t):
        out_ref[l, :, s * C:(s + 1) * C] = sol_t.astype(F32).T.astype(BF16)
        if s == 1:
            out_copy(l).start()

    def up_copy(t, s, d):
        slot = upper.at[t, s, core, z]
        return remote(slot, slot, up_s.at[t, s], up_r.at[t, s, d - 1], z_peer(d))

    def forward_copy(t, s, d):
        slot = upper.at[t, s, core, (z - d) % 4]
        return remote(slot, slot, fw_s.at[t, s], fw_r.at[t, s, d], sibling)

    def part_copy(t, s, h, du, dv):
        u, v = axes(h)
        return remote(
            part_out.at[t, s, h, du, dv], part_in.at[t, s, h, du, dv],
            p1_s.at[t, s], p1_r.at[t, s, h, du, dv], (row_of(h, u + du, v), col),
        )

    def line_copy(t, s, h, dv):
        u, v = axes(h)
        return remote(
            line_out.at[t, s, h, dv], line_in.at[t, s, h, dv],
            p2_s.at[t, s], p2_r.at[t, s, h, dv], (row_of(h, u, v + dv), col),
        )

    def up_send(t, s):
        for d in (2, 1, 3):
            up_copy(t, s, d).start()
        forward_copy(t, s, 0).start()

    def up_forward(t, s):
        for d in (1, 3, 2):
            slot = upper.at[t, s, core, (z - d) % 4]
            remote(slot, slot, up_s.at[t, s], up_r.at[t, s, d - 1], sibling).wait_recv()
            forward_copy(t, s, d).start()

    def up_parts(t, s):
        for d in (0, 1, 3, 2):
            slot = upper.at[t, s, other, (z - d) % 4]
            remote(slot, slot, fw_s.at[t, s], fw_r.at[t, s, d], sibling).wait_recv()
        left = jnp.concatenate([upper[t, s, c, r] for c in range(2) for r in range(4)], axis=1)
        pairs = [((2, 2), (2, 1)), ((2, 3), (1, 2)), ((3, 2), (1, 1)), ((1, 3), (3, 1)),
                 ((3, 3), (0, 2)), ((2, 0), (0, 1)), ((1, 0), (0, 3)), ((3, 0), (0, 0))]
        for two in pairs:
            slots = [row_of(0, x + a, y + b) for a, b in two]
            right = jnp.concatenate([wd[2 - t, p].reshape(8 * B, B) for p in slots], axis=1)
            value = dot(left, right).astype(BF16)
            for k, (a, b) in enumerate(two):
                for h in range(2):
                    du, dv = (a, b) if h == 0 else (b, a)
                    part_out[t, s, h, du, dv] = value[h * H:(h + 1) * H, k * B:(k + 1) * B]
                    if du:
                        part_copy(t, s, h, du, dv).start()

    def line_sum(t, s, h, dv):
        total = part_out[t, s, h, 0, dv].astype(F32)
        for du in (1, 3, 2):
            part_copy(t, s, h, du, dv).wait_recv()
            total = total + part_in[t, s, h, du, dv].astype(F32)
        return total

    def up_lines(t, s):
        for dv in (2, 1, 3):
            for h in range(2):
                line_out[t, s, h, dv] = line_sum(t, s, h, dv).astype(BF16)
                line_copy(t, s, h, dv).start()

    def up_finish(t, s):
        keep = []
        for h in range(2):
            total = line_sum(t, s, h, 0)
            for dv in (1, 3, 2):
                line_copy(t, s, h, dv).wait_recv()
                total = total + line_in[t, s, h, dv].astype(F32)
            keep.append(total)
        residual_t = solved_t[2 - t, s] - jnp.concatenate(keep, axis=0)
        emit(2 - t, s, finish(2 - t, t + 1, s, residual_t))

    def top(s):
        emit(3, s, finish(3, 0, s, solved_t[3, s]))

    for s in range(2):
        set_solved(0, s, ordered_ref[0, :, s * C:(s + 1) * C].astype(BF16))

    def down(l, carry):
        down_send(l, 0)

        @pl.when(l > 0)
        def _():
            down_first(l - 1, 1)
            down_second(l - 1, 1)

        down_relay(l, 0)

        @pl.when(l > 0)
        def _():
            down_finish(l - 1, 1)

        down_send(l, 1)
        down_first(l, 0)
        down_second(l, 0)
        down_relay(l, 1)
        down_finish(l, 0)
        return carry

    lax.fori_loop(0, 3, down, 0)
    top(0)

    def up(t, carry):
        up_send(t, 0)

        @pl.when(t == 0)
        def _():
            down_first(2, 1)
            down_second(2, 1)

        @pl.when(t > 0)
        def _():
            up_lines(t - 1, 1)

        up_forward(t, 0)
        up_parts(t, 0)

        @pl.when(t == 0)
        def _():
            down_finish(2, 1)
            top(1)

        @pl.when(t > 0)
        def _():
            up_finish(t - 1, 1)

        up_send(t, 1)
        up_lines(t, 0)
        up_forward(t, 1)
        up_parts(t, 1)
        up_finish(t, 0)
        return carry

    lax.fori_loop(0, 3, up, 0)
    up_lines(2, 1)
    up_finish(2, 1)

    def drain(l, carry):
        for s in range(2):
            blocks = gath.at[l, s, pl.ds(0, 15)]
            remote(blocks, blocks, ag_s.at[l, s], ag_r.at[l, s, 0, 0], sibling).wait_send()
            blocks = gath.at[l, s, pl.ds(0, 7)]
            remote(blocks, blocks, col_s.at[l, s], col_r.at[l, s, 0, 0], sibling).wait_send()
            blocks = part_out.at[l, s, :, pl.ds(0, 3)]
            remote(blocks, blocks, p1_s.at[l, s], p1_r.at[l, s, 0, 0, 0], sibling).wait_send()
            blocks = line_out.at[l, s, :, pl.ds(0, 3)]
            remote(blocks, blocks, p2_s.at[l, s], p2_r.at[l, s, 0, 0], sibling).wait_send()
            blocks = upper.at[l, s, 0, pl.ds(0, 3)]
            remote(blocks, blocks, up_s.at[l, s], up_r.at[l, s, 0], sibling).wait_send()
            blocks = upper.at[l, s, 0]
            remote(blocks, blocks, fw_s.at[l, s], fw_r.at[l, s, 0], sibling).wait_send()
        return carry

    lax.fori_loop(0, 3, drain, 0)
    for l in range(NLEV):
        out_copy(l).wait()
    all_rows.wait_send()
    all_meta.wait_send()
    meta_swap.wait_send()
    mix_swap.wait_send()


def solve(rhs, dest, diag, mask, lower):
    hbm = pl.BlockSpec(memory_space=pltpu.HBM)
    dma = pltpu.SemaphoreType.DMA
    return pl.pallas_call(
        solve_kernel,
        out_shape=jax.ShapeDtypeStruct((NLEV, B, N), BF16),
        in_specs=[hbm] * 5,
        out_specs=pl.BlockSpec(memory_space=pl.ANY),
        scratch_shapes=[
            pltpu.SemaphoreType.REGULAR,
            pltpu.VMEM(rhs.shape, F32),
            pltpu.VMEM(dest.shape, jnp.int32),
            pltpu.VMEM(diag.shape, BF16),
            pltpu.SMEM(mask.shape, jnp.int32),
            pltpu.VMEM((NLEV, B, N), BF16),
            pltpu.VMEM((64, 8, N), BF16),
            pltpu.VMEM((64, 8, N), BF16),
            pltpu.VMEM((64, 1, B), F32),
            pltpu.VMEM((64, 1, B), F32),
            pltpu.VMEM((64, 1, B), F32),
            pltpu.VMEM((256, N), BF16),
            pltpu.VMEM((256, N), BF16),
            pltpu.VMEM((NLEV, B, N), F32),
            pltpu.VMEM((3, 8, B, 16, B), BF16),
            pltpu.VMEM((3, 16, 2, 4, B, B), BF16),
            pltpu.VMEM((4, 2, 16, B, C), BF16),
            pltpu.VMEM((2, 2, 4, B, C), F32),
            pltpu.VMEM((3, 2, 2, 4, B, C), BF16),
            pltpu.VMEM((3, 2, 2, 4, B, C), BF16),
            pltpu.VMEM((4, 2, C, B), F32),
            pltpu.VMEM((4, 2, 2, 4, C, B), BF16),
            pltpu.VMEM((3, 2, 2, 4, 4, H, B), BF16),
            pltpu.VMEM((3, 2, 2, 4, 4, H, B), BF16),
            pltpu.VMEM((3, 2, 2, 4, H, B), BF16),
            pltpu.VMEM((3, 2, 2, 4, H, B), BF16),
            dma, dma, dma, dma, dma((2,)), dma((2,)),
            dma((4,)), dma((3,)), dma((NLEV,)), dma((3, 2)), dma((3, 2, 2, 15)), dma((3, 2)), dma((3, 2, 2, 4)),
            dma((3, 2)), dma((3, 2, 3)), dma((3, 2)), dma((3, 2, 4)),
            dma((3, 2)), dma((3, 2, 2, 4, 4)), dma((3, 2)), dma((3, 2, 2, 4)),
        ],
        compiler_params=pltpu.CompilerParams(
            collective_id=0, has_side_effects=True, vmem_limit_bytes=50 * 1024 * 1024
        ),
    )(*[pltpu.with_memory_space_constraint(a, pltpu.HBM) for a in (rhs, dest, diag, mask, lower)])


def per_device(rhs_rows, dest_row, diag_inverse, lower_blocks, block_mask):
    dest = dest_row.reshape(1, dest_row.shape[0])
    return solve(rhs_rows, dest, diag_inverse[:, 0], block_mask, lower_blocks)[:, None]


def solution(mesh):
    in_specs = (
        P(("row", "col"), None),
        P(("row", "col")),
        P(None, ("row", "col"), None, None),
        P(None, "row", None, None, "col", None, None),
        P(None, "row", None, "col", None),
    )
    out_specs = P(None, ("row", "col"), None, None)
    return jax.shard_map(per_device, mesh=mesh, in_specs=in_specs, out_specs=out_specs, check_vma=False)
```

```python
import jax
import jax.numpy as jnp
from jax import lax
from jax.experimental import pallas as pl
from jax.experimental.pallas import tpu as pltpu
from jax.sharding import PartitionSpec as P

B = 128
NLEV = 4
N = 256
C = 128
H = 64
MESH = pl.DeviceIdType.MESH
F32 = jnp.float32
BF16 = jnp.bfloat16


def dot(a, b):
    return jnp.dot(a, b, preferred_element_type=F32)


def dot_rows(a, b):
    return lax.dot_general(a, b, (((1,), (1,)), ((), ())), preferred_element_type=F32)


def one_hot(condition):
    return jnp.where(condition, 1.0, 0.0).astype(BF16)


def iota(shape, axis):
    return lax.broadcasted_iota(jnp.int32, shape, axis)


def solve_kernel(
    rhs_hbm, dest_hbm, diag_hbm, mask_hbm, w_hbm, out_hbm,
    hello, rhs_ref, dest_ref, diag_ref, mask_ref, out_ref,     rows_out, rows_in, meta_out, meta_in, meta_sib, mix_out, mix_in, mixer, placer, ordered_ref, raw, wd, gath, acc, col_out, col_in, solved_t, upper, part_out, part_in, line_out, line_in,
    rows_s, rows_r, meta_s, meta_r, mix_s, mix_r, in_sem, load_sem, out_sem, ag_s, ag_r, col_s, col_r, up_s, up_r, fw_s, fw_r, p1_s, p1_r, p2_s, p2_r,
):
    row = lax.axis_index("row")
    col = lax.axis_index("col")
    x, y = row // 4, row % 4
    z, core = col // 2, col % 2
    other = 1 - core

    def row_of(h, u, v):
        return (u % 4) * 4 + v % 4 if h == 0 else (v % 4) * 4 + u % 4

    def remote(src, dst, ssem, rsem, dev):
        return pltpu.make_async_remote_copy(
            src_ref=src, dst_ref=dst, send_sem=ssem, recv_sem=rsem, device_id=dev, device_id_type=MESH
        )

    sibling = (row, z * 2 + other)

    def z_peer(d):
        return (row, ((z + d) % 4) * 2 + core)

    chip = row * 4 + z

    def chip_peer(k):
        t = (chip + k) % 64
        return t, (t // 4, (t % 4) * 2 + core)

    def line(axis):
        if axis == "x":
            return [(row_of(0, x + d, y), col) for d in (1, 2, 3)]
        return [(row_of(0, x, y + d), col) for d in (1, 2, 3)]

    inputs = [(dest_hbm, dest_ref), (rhs_hbm, rhs_ref), (mask_hbm, mask_ref), (diag_hbm, diag_ref)]
    inputs = [pltpu.make_async_copy(src, dst, in_sem.at[i]) for i, (src, dst) in enumerate(inputs)]
    for copy in inputs:
        copy.start()
    near = [(row_of(0, x + a, y), ((z + b) % 4) * 2 + core) for a in range(4) for b in range(4) if a or b]
    near += line("y") + [sibling]
    barrier = pltpu.get_barrier_semaphore()
    for dev in near:
        pl.semaphore_signal(barrier, inc=1, device_id=dev, device_id_type=MESH)

    loads = [pltpu.make_async_copy(w_hbm.at[l, 0, :, :, 0], raw.at[l], load_sem.at[l]) for l in range(3)]

    def loads_wait(l):
        pltpu.make_async_copy(w_hbm.at[l, 0, :, :, 0], raw.at[l], load_sem.at[l]).wait()

    out_row, in_row = iota((256, 256), 0), iota((256, 256), 1)
    perm = one_hot(in_row == (out_row & 15) * 16 + (out_row >> 4))

    def relayout(l):
        def one(i, carry):
            zz, cc = i // 2, i % 2
            scale = [mask_ref[l, 0, i, 0, p].astype(F32) for p in range(16)]
            for k0 in range(0, 8, 2):
                piece = jnp.concatenate(
                    [raw[l, i, (k0 + s) * 16:(k0 + s + 1) * 16].reshape(256, B) for s in range(2)], axis=1
                )
                moved = dot(perm, piece)
                for p in range(16):
                    for s in range(2):
                        tile = moved[p * 16:(p + 1) * 16, s * B:(s + 1) * B] * scale[p]
                        wd[l, p, cc, zz, (k0 + s) * 16:(k0 + s + 1) * 16, :] = tile.astype(BF16)
            return carry

        lax.fori_loop(0, 8, one, 0)

    def prepare(l, carry):
        loads_wait(l)
        relayout(l)
        return carry

    for copy in inputs[:2]:
        copy.wait()
    for load in loads:
        load.start()
    dest = dest_ref[...]
    owner = (dest >> 7) & 127
    place = (dest >> 14) * B + (dest & 127)
    owned = one_hot(iota((128, 512), 0) == owner)
    before = dot(owned, one_hot(iota((512, 512), 0) < iota((512, 512), 1)))
    rank = jnp.sum(owned.astype(F32) * before, axis=0, keepdims=True)
    slot = owner * 4 + rank.astype(jnp.int32)
    sort = one_hot(iota((512, 512), 0) == slot)
    rows_out[...] = dot(sort, rhs_ref[...].astype(BF16)).astype(BF16).reshape(64, 8, N)
    lane = iota((128, 512), 0)
    digit = jnp.where(lane < 8, place >> 4, place & 15)
    digit = jnp.where((lane < 16) & ((lane & 7) == (slot & 7)), digit, 0).astype(F32).astype(BF16)
    meta_out[...] = dot_rows(one_hot(iota((64, 512), 0) == (slot >> 3)), digit).reshape(64, 1, B)

    def rows_copy(t, dev):
        return remote(rows_out.at[t], rows_in.at[chip], rows_s, rows_r, dev)

    def meta_copy(t, dev):
        return remote(meta_out.at[t], meta_in.at[chip], meta_s, meta_r, dev)

    pl.semaphore_wait(barrier, len(near))
    for dev in line("y"):
        pl.semaphore_signal(hello, inc=1, device_id=dev, device_id_type=MESH)
    for copy in inputs[2:]:
        copy.wait()
    prepare(0, 0)
    pl.semaphore_wait(hello, 3)

    def send_rows(k, carry):
        t, dev = chip_peer(k)
        meta_copy(t, dev).start()
        rows_copy(t, dev).start()
        return carry

    lax.fori_loop(1, 64, send_rows, 0)
    rows_in[chip] = rows_out[chip]
    meta_in[chip] = meta_out[chip]

    lax.fori_loop(1, 3, prepare, 0)

    some = pl.ds(0, 63)
    all_rows = remote(rows_out.at[some], rows_in.at[some], rows_s, rows_r, sibling)
    all_meta = remote(meta_out.at[some], meta_in.at[some], meta_s, meta_r, sibling)
    to, at = iota((512, 512), 0), iota((512, 512), 1)
    half = jnp.where(to < 256, core, other)
    mixer[...] = one_hot(at == (to & 63) * 8 + half * 4 + ((to >> 6) & 3))

    def places(meta):
        digits = jnp.concatenate([meta.reshape(64, B)] * 4, axis=0)
        at_lane, k = iota((256, B), 1), iota((256, B), 0) >> 6
        mine = (at_lane < 16) & ((at_lane & 7) == core * 4 + k)
        weight = jnp.where(iota((8, B), 1) < 8, 16.0, 1.0).astype(BF16)
        where = dot_rows(weight, jnp.where(mine, digits, 0.0).astype(BF16))[:1]
        return one_hot(iota((512, 256), 0) == where.astype(jnp.int32))

    all_meta.wait_recv()
    meta_swap = remote(meta_in, meta_sib, mix_s.at[0], mix_r.at[0], sibling)
    meta_swap.start()
    placer[0] = places(meta_in[...])
    meta_swap.wait_recv()
    placer[1] = places(meta_sib[...])
    all_rows.wait_recv()
    arrived = rows_in[...].reshape(512, N)
    mix_out[...] = dot(mixer[256:], arrived).astype(BF16)
    mix_swap = remote(mix_out, mix_in, mix_s.at[1], mix_r.at[1], sibling)
    mix_swap.start()
    total = dot(placer[0], dot(mixer[:256], arrived).astype(BF16))
    mix_swap.wait_recv()
    ordered_ref[...] = (total + dot(placer[1], mix_in[...])).reshape(NLEV, B, N)

    def set_solved(l, s, residual):
        solved = dot(diag_ref[l], residual).astype(BF16)
        gath[l, s, row] = solved
        solved_t[l, s] = solved.astype(F32).T

    def axes(h):
        return (x, y) if h == 0 else (y, x)

    order = [(a, b) for a in (0, 1, 3) for b in (0, 1, 3)] + [(a, b) for a in range(4) for b in range(4) if 2 in (a, b)]

    def batch_of(h, e, d):
        return 6 if ((e, d) if h == 0 else (d, e)) in order[:8] else 7

    def gather_copy(l, s, h, slot, e, d, dev):
        sem = batch_of(h, e, d) if d else h * 3 + e - 1
        rows = gath.at[l, s, slot, pl.ds(h * H, H)]
        return remote(rows, rows, ag_s.at[l, s], ag_r.at[l, s, sem], dev)

    def relay(l, s, h, e):
        u, v = axes(h)
        slot = row_of(h, u - e, v)
        if e:
            gather_copy(l, s, h, slot, e, 0, (row, col)).wait_recv()
        for d in (2, 1, 3):
            gather_copy(l, s, h, slot, e, d, (row_of(h, u, v + d), col)).start()

    def down_send(l, s):
        for h in range(2):
            u, v = axes(h)
            for d in (2, 1, 3):
                gather_copy(l, s, h, row, d, 0, (row_of(h, u + d, v), col)).start()
        for h in range(2):
            relay(l, s, h, 0)

    def down_relay(l, s):
        for e in (1, 3, 2):
            for h in range(2):
                relay(l, s, h, e)

    def operands(l, s, batch):
        some = order[8 * batch:8 * batch + 8]
        halves = sum((a != 0) + (b != 0) for a, b in some)
        blocks = gath.at[l, s, pl.ds(0, halves // 2)]
        remote(blocks, blocks, ag_s.at[l, s], ag_r.at[l, s, 6 + batch], sibling).wait_recv()
        slots = [row_of(0, x - a, y - b) for a, b in some]
        return slots, jnp.concatenate([gath[l, s, p] for p in slots], axis=0)

    def down_first(l, s):
        slots, rhs = operands(l, s, 0)
        for c in range(2):
            for r in range(0, 4, 2):
                left = jnp.concatenate([wd[l, p, c, r:r + 2].reshape(2 * B, B) for p in slots], axis=1)
                acc[s, c, r:r + 2] = dot(left, rhs).reshape(2, B, C)

    def col_copy(l, s, dc, zz):
        d = (zz - z + 4) % 4
        return remote(
            col_out.at[l, s, dc, zz], col_in.at[l, s, dc, d], col_s.at[l, s], col_r.at[l, s],
            (row, zz * 2 + (other if dc else core)),
        )

    def down_second(l, s):
        slots, rhs = operands(l, s, 1)
        for half in range(2):
            r = ((z // 2 + 1 - half) % 2) * 2
            for dc, c in ((1, other), (0, core)):
                left = jnp.concatenate([wd[l, p, c, pl.ds(r, 2)].reshape(2 * B, B) for p in slots], axis=1)
                total = acc[s, c, pl.ds(r, 2)] + dot(left, rhs).reshape(2, B, C)
                col_out[l, s, dc, pl.ds(r, 2)] = total.astype(BF16)
                if half == 0 or dc == 1:
                    col_copy(l, s, dc, r + z % 2).start()
                else:
                    acc[s, c, pl.ds(r, 2)] = total
                col_copy(l, s, dc, r + 1 - z % 2).start()

    def down_finish(l, s):
        own = ordered_ref[l + 1, :, s * C:(s + 1) * C] - acc[s, core, z]
        blocks = gath.at[l, s, pl.ds(0, 7)]
        remote(blocks, blocks, col_s.at[l, s], col_r.at[l, s], sibling).wait_recv()
        for dc in range(2):
            for d in range(1 - dc, 4):
                own = own - col_in[l, s, dc, d].astype(F32)
        set_solved(l + 1, s, own.astype(BF16))

    def out_copy(l):
        return pltpu.make_async_copy(out_ref.at[l], out_hbm.at[l], out_sem.at[l])

    def finish(l, slot, s, residual_t):
        sol_t = dot(residual_t.astype(BF16), diag_ref[l]).astype(BF16)
        upper[slot, s, core, z] = sol_t
        return sol_t

    def emit(l, s, sol_t):
        out_ref[l, :, s * C:(s + 1) * C] = sol_t.astype(F32).T.astype(BF16)
        if s == 1:
            out_copy(l).start()

    def up_copy(t, s, d):
        slot = upper.at[t, s, core, z]
        return remote(slot, slot, up_s.at[t, s], up_r.at[t, s, d - 1], z_peer(d))

    def forward_copy(t, s, d):
        slot = upper.at[t, s, core, (z - d) % 4]
        return remote(slot, slot, fw_s.at[t, s], fw_r.at[t, s], sibling)

    def part_copy(t, s, h, du, dv):
        u, v = axes(h)
        return remote(
            part_out.at[t, s, h, du, dv], part_in.at[t, s, h, du, dv],
            p1_s.at[t, s], p1_r.at[t, s, dv], (row_of(h, u + du, v), col),
        )

    def line_copy(t, s, h, dv):
        u, v = axes(h)
        return remote(
            line_out.at[t, s, h, dv], line_in.at[t, s, h, dv],
            p2_s.at[t, s], p2_r.at[t, s], (row_of(h, u, v + dv), col),
        )

    def up_send(t, s):
        for d in (2, 1, 3):
            up_copy(t, s, d).start()
        forward_copy(t, s, 0).start()

    def up_forward(t, s):
        for d in (1, 3, 2):
            slot = upper.at[t, s, core, (z - d) % 4]
            remote(slot, slot, up_s.at[t, s], up_r.at[t, s, d - 1], sibling).wait_recv()
            forward_copy(t, s, d).start()

    def up_parts(t, s):
        slot = upper.at[t, s, other]
        remote(slot, slot, fw_s.at[t, s], fw_r.at[t, s], sibling).wait_recv()
        left = jnp.concatenate([upper[t, s, c, r] for c in range(2) for r in range(4)], axis=1)
        pairs = [((2, 2), (2, 1)), ((2, 3), (1, 2)), ((3, 2), (1, 1)), ((1, 3), (3, 1)),
                 ((3, 3), (0, 2)), ((2, 0), (0, 1)), ((1, 0), (0, 3)), ((3, 0), (0, 0))]
        for two in pairs:
            slots = [row_of(0, x + a, y + b) for a, b in two]
            right = jnp.concatenate([wd[2 - t, p].reshape(8 * B, B) for p in slots], axis=1)
            value = dot(left, right).astype(BF16)
            for k, (a, b) in enumerate(two):
                for h in range(2):
                    du, dv = (a, b) if h == 0 else (b, a)
                    part_out[t, s, h, du, dv] = value[h * H:(h + 1) * H, k * B:(k + 1) * B]
                    if du:
                        part_copy(t, s, h, du, dv).start()

    def line_sums(t, s, dv):
        blocks = part_in.at[t, s, :, pl.ds(0, 3), 0]
        remote(blocks, blocks, p1_s.at[t, s], p1_r.at[t, s, dv], sibling).wait_recv()
        sums = []
        for h in range(2):
            total = part_out[t, s, h, 0, dv].astype(F32)
            for du in (1, 3, 2):
                total = total + part_in[t, s, h, du, dv].astype(F32)
            sums.append(total)
        return sums

    def up_lines(t, s):
        for dv in (2, 1, 3):
            for h, total in enumerate(line_sums(t, s, dv)):
                line_out[t, s, h, dv] = total.astype(BF16)
                line_copy(t, s, h, dv).start()

    def up_finish(t, s):
        keep = line_sums(t, s, 0)
        blocks = line_in.at[t, s, :, pl.ds(0, 3)]
        remote(blocks, blocks, p2_s.at[t, s], p2_r.at[t, s], sibling).wait_recv()
        for h in range(2):
            for dv in (1, 3, 2):
                keep[h] = keep[h] + line_in[t, s, h, dv].astype(F32)
        residual_t = solved_t[2 - t, s] - jnp.concatenate(keep, axis=0)
        emit(2 - t, s, finish(2 - t, t + 1, s, residual_t))

    def top(s):
        emit(3, s, finish(3, 0, s, solved_t[3, s]))

    for s in range(2):
        set_solved(0, s, ordered_ref[0, :, s * C:(s + 1) * C].astype(BF16))

    def down(l, carry):
        down_send(l, 0)

        @pl.when(l > 0)
        def _():
            down_first(l - 1, 1)
            down_second(l - 1, 1)

        down_relay(l, 0)

        @pl.when(l > 0)
        def _():
            down_finish(l - 1, 1)

        down_send(l, 1)
        down_first(l, 0)
        down_second(l, 0)
        down_relay(l, 1)
        down_finish(l, 0)
        return carry

    lax.fori_loop(0, 3, down, 0)
    top(0)

    def up(t, carry):
        up_send(t, 0)

        @pl.when(t == 0)
        def _():
            down_first(2, 1)
            down_second(2, 1)

        @pl.when(t > 0)
        def _():
            up_lines(t - 1, 1)

        up_forward(t, 0)
        up_parts(t, 0)

        @pl.when(t == 0)
        def _():
            down_finish(2, 1)
            top(1)

        @pl.when(t > 0)
        def _():
            up_finish(t - 1, 1)

        up_send(t, 1)
        up_lines(t, 0)
        up_forward(t, 1)
        up_parts(t, 1)
        up_finish(t, 0)
        return carry

    lax.fori_loop(0, 3, up, 0)
    up_lines(2, 1)
    up_finish(2, 1)

    def drain(l, carry):
        for s in range(2):
            blocks = gath.at[l, s, pl.ds(0, 15)]
            remote(blocks, blocks, ag_s.at[l, s], ag_r.at[l, s, 0], sibling).wait_send()
            blocks = gath.at[l, s, pl.ds(0, 7)]
            remote(blocks, blocks, col_s.at[l, s], col_r.at[l, s], sibling).wait_send()
            blocks = part_out.at[l, s, :, pl.ds(0, 3)]
            remote(blocks, blocks, p1_s.at[l, s], p1_r.at[l, s, 0], sibling).wait_send()
            blocks = line_out.at[l, s, :, pl.ds(0, 3)]
            remote(blocks, blocks, p2_s.at[l, s], p2_r.at[l, s], sibling).wait_send()
            blocks = upper.at[l, s, 0, pl.ds(0, 3)]
            remote(blocks, blocks, up_s.at[l, s], up_r.at[l, s, 0], sibling).wait_send()
            blocks = upper.at[l, s, 0]
            remote(blocks, blocks, fw_s.at[l, s], fw_r.at[l, s], sibling).wait_send()
        return carry

    lax.fori_loop(0, 3, drain, 0)
    for l in range(NLEV):
        out_copy(l).wait()
    all_rows.wait_send()
    all_meta.wait_send()
    meta_swap.wait_send()
    mix_swap.wait_send()


def solve(rhs, dest, diag, mask, lower):
    hbm = pl.BlockSpec(memory_space=pltpu.HBM)
    dma = pltpu.SemaphoreType.DMA
    return pl.pallas_call(
        solve_kernel,
        out_shape=jax.ShapeDtypeStruct((NLEV, B, N), BF16),
        in_specs=[hbm] * 5,
        out_specs=pl.BlockSpec(memory_space=pl.ANY),
        scratch_shapes=[
            pltpu.SemaphoreType.REGULAR,
            pltpu.VMEM(rhs.shape, F32),
            pltpu.VMEM(dest.shape, jnp.int32),
            pltpu.VMEM(diag.shape, BF16),
            pltpu.SMEM(mask.shape, jnp.int32),
            pltpu.VMEM((NLEV, B, N), BF16),
            pltpu.VMEM((64, 8, N), BF16),
            pltpu.VMEM((64, 8, N), BF16),
            pltpu.VMEM((64, 1, B), F32),
            pltpu.VMEM((64, 1, B), F32),
            pltpu.VMEM((64, 1, B), F32),
            pltpu.VMEM((256, N), BF16),
            pltpu.VMEM((256, N), BF16),
            pltpu.VMEM((512, 512), BF16),
            pltpu.VMEM((2, 512, 256), BF16),
            pltpu.VMEM((NLEV, B, N), F32),
            pltpu.VMEM((3, 8, B, 16, B), BF16),
            pltpu.VMEM((3, 16, 2, 4, B, B), BF16),
            pltpu.VMEM((4, 2, 16, B, C), BF16),
            pltpu.VMEM((2, 2, 4, B, C), F32),
            pltpu.VMEM((3, 2, 2, 4, B, C), BF16),
            pltpu.VMEM((3, 2, 2, 4, B, C), BF16),
            pltpu.VMEM((4, 2, C, B), F32),
            pltpu.VMEM((4, 2, 2, 4, C, B), BF16),
            pltpu.VMEM((3, 2, 2, 4, 4, H, B), BF16),
            pltpu.VMEM((3, 2, 2, 4, 4, H, B), BF16),
            pltpu.VMEM((3, 2, 2, 4, H, B), BF16),
            pltpu.VMEM((3, 2, 2, 4, H, B), BF16),
            dma, dma, dma, dma, dma((2,)), dma((2,)),
            dma((4,)), dma((3,)), dma((NLEV,)), dma((3, 2)), dma((3, 2, 8)), dma((3, 2)), dma((3, 2)),
            dma((3, 2)), dma((3, 2, 3)), dma((3, 2)), dma((3, 2)), dma((3, 2)), dma((3, 2, 4)), dma((3, 2)), dma((3, 2)),
        ],
        compiler_params=pltpu.CompilerParams(
            collective_id=0, has_side_effects=True, vmem_limit_bytes=50 * 1024 * 1024
        ),
    )(*[pltpu.with_memory_space_constraint(a, pltpu.HBM) for a in (rhs, dest, diag, mask, lower)])


def per_device(rhs_rows, dest_row, diag_inverse, lower_blocks, block_mask):
    dest = dest_row.reshape(1, dest_row.shape[0])
    return solve(rhs_rows, dest, diag_inverse[:, 0], block_mask, lower_blocks)[:, None]


def solution(mesh):
    in_specs = (
        P(("row", "col"), None),
        P(("row", "col")),
        P(None, ("row", "col"), None, None),
        P(None, "row", None, None, "col", None, None),
        P(None, "row", None, "col", None),
    )
    out_specs = P(None, ("row", "col"), None, None)
    return jax.shard_map(per_device, mesh=mesh, in_specs=in_specs, out_specs=out_specs, check_vma=False)
```

```python
import jax
import jax.numpy as jnp
from jax import lax
from jax.experimental import pallas as pl
from jax.experimental.pallas import tpu as pltpu
from jax.sharding import PartitionSpec as P

B = 128
NLEV = 4
N = 256
C = 128
H = 64
MESH = pl.DeviceIdType.MESH
F32 = jnp.float32
BF16 = jnp.bfloat16


def dot(a, b):
    return jnp.dot(a, b, preferred_element_type=F32)


def dot_rows(a, b):
    return lax.dot_general(a, b, (((1,), (1,)), ((), ())), preferred_element_type=F32)


def one_hot(condition):
    return jnp.where(condition, 1.0, 0.0).astype(BF16)


def iota(shape, axis):
    return lax.broadcasted_iota(jnp.int32, shape, axis)


def solve_kernel(
    rhs_hbm, dest_hbm, diag_hbm, mask_hbm, w_hbm, out_hbm,
    hello, rhs_ref, dest_ref, diag_ref, mask_ref, out_ref,     rows_out, rows_in, meta_out, meta_in, meta_sib, mix_out, mix_in, mixer, placer, ordered_ref, raw, wd, gath, acc, col_out, col_in, solved_t, upper, part_out, part_in, line_out, line_in,
    rows_s, rows_r, meta_s, meta_r, mix_s, mix_r, in_sem, load_sem, out_sem, ag_s, ag_r, col_s, col_r, up_s, up_r, fw_s, fw_r, p1_s, p1_r, p2_s, p2_r,
):
    row = lax.axis_index("row")
    col = lax.axis_index("col")
    x, y = row // 4, row % 4
    z, core = col // 2, col % 2
    other = 1 - core

    def row_of(h, u, v):
        return (u % 4) * 4 + v % 4 if h == 0 else (v % 4) * 4 + u % 4

    def remote(src, dst, ssem, rsem, dev):
        return pltpu.make_async_remote_copy(
            src_ref=src, dst_ref=dst, send_sem=ssem, recv_sem=rsem, device_id=dev, device_id_type=MESH
        )

    sibling = (row, z * 2 + other)

    def z_peer(d):
        return (row, ((z + d) % 4) * 2 + core)

    chip = row * 4 + z

    def chip_peer(k):
        t = (chip + k) % 64
        return t, (t // 4, (t % 4) * 2 + core)

    def line(axis):
        if axis == "x":
            return [(row_of(0, x + d, y), col) for d in (1, 2, 3)]
        return [(row_of(0, x, y + d), col) for d in (1, 2, 3)]

    inputs = [(dest_hbm, dest_ref), (rhs_hbm, rhs_ref), (mask_hbm, mask_ref), (diag_hbm, diag_ref)]
    inputs = [pltpu.make_async_copy(src, dst, in_sem.at[i]) for i, (src, dst) in enumerate(inputs)]
    for copy in inputs:
        copy.start()
    near = [(row_of(0, x + a, y), ((z + b) % 4) * 2 + core) for a in range(4) for b in range(4) if a or b]
    near += line("y") + [sibling]
    barrier = pltpu.get_barrier_semaphore()
    for dev in near:
        pl.semaphore_signal(barrier, inc=1, device_id=dev, device_id_type=MESH)

    loads = [pltpu.make_async_copy(w_hbm.at[l, 0, :, :, 0], raw.at[l], load_sem.at[l]) for l in range(3)]

    def loads_wait(l):
        pltpu.make_async_copy(w_hbm.at[l, 0, :, :, 0], raw.at[l], load_sem.at[l]).wait()

    out_row, in_row = iota((256, 256), 0), iota((256, 256), 1)
    perm = one_hot(in_row == (out_row & 15) * 16 + (out_row >> 4))

    def relayout(l):
        def one(i, carry):
            zz, cc = i // 2, i % 2
            scale = [mask_ref[l, 0, i, 0, p].astype(F32) for p in range(16)]
            for k0 in range(0, 8, 2):
                piece = jnp.concatenate(
                    [raw[l, i, (k0 + s) * 16:(k0 + s + 1) * 16].reshape(256, B) for s in range(2)], axis=1
                )
                moved = dot(perm, piece)
                for p in range(16):
                    for s in range(2):
                        tile = moved[p * 16:(p + 1) * 16, s * B:(s + 1) * B] * scale[p]
                        wd[l, p, cc, zz, (k0 + s) * 16:(k0 + s + 1) * 16, :] = tile.astype(BF16)
            return carry

        lax.fori_loop(0, 8, one, 0)

    def prepare(l, carry):
        loads_wait(l)
        relayout(l)
        return carry

    for copy in inputs[:2]:
        copy.wait()
    for load in loads:
        load.start()
    dest = dest_ref[...]
    owner = (dest >> 7) & 127
    place = (dest >> 14) * B + (dest & 127)
    owned = one_hot(iota((128, 512), 0) == owner)
    before = dot(owned, one_hot(iota((512, 512), 0) < iota((512, 512), 1)))
    rank = jnp.sum(owned.astype(F32) * before, axis=0, keepdims=True)
    slot = owner * 4 + rank.astype(jnp.int32)
    sort = one_hot(iota((512, 512), 0) == slot)
    rows_out[...] = dot(sort, rhs_ref[...].astype(BF16)).astype(BF16).reshape(64, 8, N)
    lane = iota((128, 512), 0)
    digit = jnp.where(lane < 8, place >> 4, place & 15)
    digit = jnp.where((lane < 16) & ((lane & 7) == (slot & 7)), digit, 0).astype(F32).astype(BF16)
    meta_out[...] = dot_rows(one_hot(iota((64, 512), 0) == (slot >> 3)), digit).reshape(64, 1, B)

    def rows_copy(t, dev):
        return remote(rows_out.at[t], rows_in.at[chip], rows_s, rows_r, dev)

    def meta_copy(t, dev):
        return remote(meta_out.at[t], meta_in.at[chip], meta_s, meta_r, dev)

    pl.semaphore_wait(barrier, len(near))
    for dev in line("y"):
        pl.semaphore_signal(hello, inc=1, device_id=dev, device_id_type=MESH)
    for copy in inputs[2:]:
        copy.wait()
    pl.semaphore_wait(hello, 3)

    def send_rows(k, carry):
        t, dev = chip_peer(k)
        meta_copy(t, dev).start()
        rows_copy(t, dev).start()
        return carry

    lax.fori_loop(1, 64, send_rows, 0)
    rows_in[chip] = rows_out[chip]
    meta_in[chip] = meta_out[chip]

    prepare(0, 0)

    some = pl.ds(0, 63)
    all_rows = remote(rows_out.at[some], rows_in.at[some], rows_s, rows_r, sibling)
    all_meta = remote(meta_out.at[some], meta_in.at[some], meta_s, meta_r, sibling)
    to, at = iota((512, 512), 0), iota((512, 512), 1)
    half = jnp.where(to < 256, core, other)
    mixer[...] = one_hot(at == (to & 63) * 8 + half * 4 + ((to >> 6) & 3))

    def places(meta):
        digits = jnp.concatenate([meta.reshape(64, B)] * 4, axis=0)
        at_lane, k = iota((256, B), 1), iota((256, B), 0) >> 6
        mine = (at_lane < 16) & ((at_lane & 7) == core * 4 + k)
        weight = jnp.where(iota((8, B), 1) < 8, 16.0, 1.0).astype(BF16)
        where = dot_rows(weight, jnp.where(mine, digits, 0.0).astype(BF16))[:1]
        return one_hot(iota((512, 256), 0) == where.astype(jnp.int32))

    all_meta.wait_recv()
    meta_swap = remote(meta_in, meta_sib, mix_s.at[0], mix_r.at[0], sibling)
    meta_swap.start()
    placer[0] = places(meta_in[...])
    meta_swap.wait_recv()
    placer[1] = places(meta_sib[...])
    all_rows.wait_recv()
    arrived = rows_in[...].reshape(512, N)
    mix_out[...] = dot(mixer[256:], arrived).astype(BF16)
    mix_swap = remote(mix_out, mix_in, mix_s.at[1], mix_r.at[1], sibling)
    mix_swap.start()
    total = dot(placer[0], dot(mixer[:256], arrived).astype(BF16))
    mix_swap.wait_recv()
    ordered_ref[...] = (total + dot(placer[1], mix_in[...])).reshape(NLEV, B, N)

    def set_solved(l, s, residual):
        solved = dot(diag_ref[l], residual).astype(BF16)
        gath[l, s, row] = solved
        solved_t[l, s] = solved.astype(F32).T

    def axes(h):
        return (x, y) if h == 0 else (y, x)

    order = [(a, b) for a in (0, 1, 3) for b in (0, 1, 3)] + [(a, b) for a in range(4) for b in range(4) if 2 in (a, b)]

    def batch_of(h, e, d):
        return 6 if ((e, d) if h == 0 else (d, e)) in order[:8] else 7

    def gather_copy(l, s, h, slot, e, d, dev):
        sem = batch_of(h, e, d) if d else h * 3 + e - 1
        rows = gath.at[l, s, slot, pl.ds(h * H, H)]
        return remote(rows, rows, ag_s.at[l, s], ag_r.at[l, s, sem], dev)

    def relay(l, s, h, e):
        u, v = axes(h)
        slot = row_of(h, u - e, v)
        if e:
            gather_copy(l, s, h, slot, e, 0, (row, col)).wait_recv()
        for d in (2, 1, 3):
            gather_copy(l, s, h, slot, e, d, (row_of(h, u, v + d), col)).start()

    def down_send(l, s):
        for h in range(2):
            u, v = axes(h)
            for d in (2, 1, 3):
                gather_copy(l, s, h, row, d, 0, (row_of(h, u + d, v), col)).start()
        for h in range(2):
            relay(l, s, h, 0)

    def down_relay(l, s):
        for e in (1, 3, 2):
            for h in range(2):
                relay(l, s, h, e)

    def operands(l, s, batch):
        some = order[8 * batch:8 * batch + 8]
        halves = sum((a != 0) + (b != 0) for a, b in some)
        blocks = gath.at[l, s, pl.ds(0, halves // 2)]
        remote(blocks, blocks, ag_s.at[l, s], ag_r.at[l, s, 6 + batch], sibling).wait_recv()
        slots = [row_of(0, x - a, y - b) for a, b in some]
        return slots, jnp.concatenate([gath[l, s, p] for p in slots], axis=0)

    def down_first(l, s):
        slots, rhs = operands(l, s, 0)
        for c in range(2):
            for r in range(0, 4, 2):
                left = jnp.concatenate([wd[l, p, c, r:r + 2].reshape(2 * B, B) for p in slots], axis=1)
                acc[s, c, r:r + 2] = dot(left, rhs).reshape(2, B, C)

    def col_copy(l, s, dc, zz):
        d = (zz - z + 4) % 4
        return remote(
            col_out.at[l, s, dc, zz], col_in.at[l, s, dc, d], col_s.at[l, s], col_r.at[l, s],
            (row, zz * 2 + (other if dc else core)),
        )

    def down_second(l, s):
        slots, rhs = operands(l, s, 1)
        for half in range(2):
            r = ((z // 2 + 1 - half) % 2) * 2
            for dc, c in ((1, other), (0, core)):
                left = jnp.concatenate([wd[l, p, c, pl.ds(r, 2)].reshape(2 * B, B) for p in slots], axis=1)
                total = acc[s, c, pl.ds(r, 2)] + dot(left, rhs).reshape(2, B, C)
                col_out[l, s, dc, pl.ds(r, 2)] = total.astype(BF16)
                if half == 0 or dc == 1:
                    col_copy(l, s, dc, r + z % 2).start()
                else:
                    acc[s, c, pl.ds(r, 2)] = total
                col_copy(l, s, dc, r + 1 - z % 2).start()

    def down_finish(l, s):
        own = ordered_ref[l + 1, :, s * C:(s + 1) * C] - acc[s, core, z]
        blocks = gath.at[l, s, pl.ds(0, 7)]
        remote(blocks, blocks, col_s.at[l, s], col_r.at[l, s], sibling).wait_recv()
        for dc in range(2):
            for d in range(1 - dc, 4):
                own = own - col_in[l, s, dc, d].astype(F32)
        set_solved(l + 1, s, own.astype(BF16))

    def out_copy(l):
        return pltpu.make_async_copy(out_ref.at[l], out_hbm.at[l], out_sem.at[l])

    def finish(l, slot, s, residual_t):
        sol_t = dot(residual_t.astype(BF16), diag_ref[l]).astype(BF16)
        upper[slot, s, core, z] = sol_t
        return sol_t

    def emit(l, s, sol_t):
        out_ref[l, :, s * C:(s + 1) * C] = sol_t.astype(F32).T.astype(BF16)
        if s == 1:
            out_copy(l).start()

    def up_copy(t, s, d):
        slot = upper.at[t, s, core, z]
        return remote(slot, slot, up_s.at[t, s], up_r.at[t, s, d - 1], z_peer(d))

    def forward_copy(t, s, d):
        slot = upper.at[t, s, core, (z - d) % 4]
        return remote(slot, slot, fw_s.at[t, s], fw_r.at[t, s], sibling)

    def part_copy(t, s, h, du, dv):
        u, v = axes(h)
        return remote(
            part_out.at[t, s, h, du, dv], part_in.at[t, s, h, du, dv],
            p1_s.at[t, s], p1_r.at[t, s, dv], (row_of(h, u + du, v), col),
        )

    def line_copy(t, s, h, dv):
        u, v = axes(h)
        return remote(
            line_out.at[t, s, h, dv], line_in.at[t, s, h, dv],
            p2_s.at[t, s], p2_r.at[t, s], (row_of(h, u, v + dv), col),
        )

    def up_send(t, s):
        for d in (2, 1, 3):
            up_copy(t, s, d).start()
        forward_copy(t, s, 0).start()

    def up_forward(t, s):
        for d in (1, 3, 2):
            slot = upper.at[t, s, core, (z - d) % 4]
            remote(slot, slot, up_s.at[t, s], up_r.at[t, s, d - 1], sibling).wait_recv()
            forward_copy(t, s, d).start()

    def up_parts(t, s):
        slot = upper.at[t, s, other]
        remote(slot, slot, fw_s.at[t, s], fw_r.at[t, s], sibling).wait_recv()
        left = jnp.concatenate([upper[t, s, c, r] for c in range(2) for r in range(4)], axis=1)
        pairs = [((2, 2), (2, 1)), ((2, 3), (1, 2)), ((3, 2), (1, 1)), ((1, 3), (3, 1)),
                 ((3, 3), (0, 2)), ((2, 0), (0, 1)), ((1, 0), (0, 3)), ((3, 0), (0, 0))]
        for two in pairs:
            slots = [row_of(0, x + a, y + b) for a, b in two]
            right = jnp.concatenate([wd[2 - t, p].reshape(8 * B, B) for p in slots], axis=1)
            value = dot(left, right).astype(BF16)
            for k, (a, b) in enumerate(two):
                for h in range(2):
                    du, dv = (a, b) if h == 0 else (b, a)
                    part_out[t, s, h, du, dv] = value[h * H:(h + 1) * H, k * B:(k + 1) * B]
                    if du:
                        part_copy(t, s, h, du, dv).start()

    def line_sums(t, s, dv):
        blocks = part_in.at[t, s, :, pl.ds(0, 3), 0]
        remote(blocks, blocks, p1_s.at[t, s], p1_r.at[t, s, dv], sibling).wait_recv()
        sums = []
        for h in range(2):
            total = part_out[t, s, h, 0, dv].astype(F32)
            for du in (1, 3, 2):
                total = total + part_in[t, s, h, du, dv].astype(F32)
            sums.append(total)
        return sums

    def up_lines(t, s):
        for dv in (2, 1, 3):
            for h, total in enumerate(line_sums(t, s, dv)):
                line_out[t, s, h, dv] = total.astype(BF16)
                line_copy(t, s, h, dv).start()

    def up_finish(t, s):
        keep = line_sums(t, s, 0)
        blocks = line_in.at[t, s, :, pl.ds(0, 3)]
        remote(blocks, blocks, p2_s.at[t, s], p2_r.at[t, s], sibling).wait_recv()
        for h in range(2):
            for dv in (1, 3, 2):
                keep[h] = keep[h] + line_in[t, s, h, dv].astype(F32)
        residual_t = solved_t[2 - t, s] - jnp.concatenate(keep, axis=0)
        emit(2 - t, s, finish(2 - t, t + 1, s, residual_t))

    def top(s):
        emit(3, s, finish(3, 0, s, solved_t[3, s]))

    set_solved(0, 0, ordered_ref[0, :, :C].astype(BF16))

    def down(l, carry):
        down_send(l, 0)

        @pl.when(l == 0)
        def _():
            set_solved(0, 1, ordered_ref[0, :, C:].astype(BF16))
            prepare(1, 0)

        @pl.when(l > 0)
        def _():
            down_first(l - 1, 1)
            down_second(l - 1, 1)

        down_relay(l, 0)

        @pl.when(l > 0)
        def _():
            down_finish(l - 1, 1)

        down_send(l, 1)

        @pl.when(l == 0)
        def _():
            prepare(2, 0)

        down_first(l, 0)
        down_second(l, 0)
        down_relay(l, 1)
        down_finish(l, 0)
        return carry

    lax.fori_loop(0, 3, down, 0)
    top(0)

    def up(t, carry):
        up_send(t, 0)

        @pl.when(t == 0)
        def _():
            down_first(2, 1)
            down_second(2, 1)

        @pl.when(t > 0)
        def _():
            up_lines(t - 1, 1)

        up_forward(t, 0)
        up_parts(t, 0)

        @pl.when(t == 0)
        def _():
            down_finish(2, 1)
            top(1)

        @pl.when(t > 0)
        def _():
            up_finish(t - 1, 1)

        up_send(t, 1)
        up_lines(t, 0)
        up_forward(t, 1)
        up_parts(t, 1)
        up_finish(t, 0)
        return carry

    lax.fori_loop(0, 3, up, 0)
    up_lines(2, 1)
    up_finish(2, 1)

    def drain(l, carry):
        for s in range(2):
            blocks = gath.at[l, s, pl.ds(0, 15)]
            remote(blocks, blocks, ag_s.at[l, s], ag_r.at[l, s, 0], sibling).wait_send()
            blocks = gath.at[l, s, pl.ds(0, 7)]
            remote(blocks, blocks, col_s.at[l, s], col_r.at[l, s], sibling).wait_send()
            blocks = part_out.at[l, s, :, pl.ds(0, 3)]
            remote(blocks, blocks, p1_s.at[l, s], p1_r.at[l, s, 0], sibling).wait_send()
            blocks = line_out.at[l, s, :, pl.ds(0, 3)]
            remote(blocks, blocks, p2_s.at[l, s], p2_r.at[l, s], sibling).wait_send()
            blocks = upper.at[l, s, 0, pl.ds(0, 3)]
            remote(blocks, blocks, up_s.at[l, s], up_r.at[l, s, 0], sibling).wait_send()
            blocks = upper.at[l, s, 0]
            remote(blocks, blocks, fw_s.at[l, s], fw_r.at[l, s], sibling).wait_send()
        return carry

    lax.fori_loop(0, 3, drain, 0)
    for l in range(NLEV):
        out_copy(l).wait()
    all_rows.wait_send()
    all_meta.wait_send()
    meta_swap.wait_send()
    mix_swap.wait_send()


def solve(rhs, dest, diag, mask, lower):
    hbm = pl.BlockSpec(memory_space=pltpu.HBM)
    dma = pltpu.SemaphoreType.DMA
    return pl.pallas_call(
        solve_kernel,
        out_shape=jax.ShapeDtypeStruct((NLEV, B, N), BF16),
        in_specs=[hbm] * 5,
        out_specs=pl.BlockSpec(memory_space=pl.ANY),
        scratch_shapes=[
            pltpu.SemaphoreType.REGULAR,
            pltpu.VMEM(rhs.shape, F32),
            pltpu.VMEM(dest.shape, jnp.int32),
            pltpu.VMEM(diag.shape, BF16),
            pltpu.SMEM(mask.shape, jnp.int32),
            pltpu.VMEM((NLEV, B, N), BF16),
            pltpu.VMEM((64, 8, N), BF16),
            pltpu.VMEM((64, 8, N), BF16),
            pltpu.VMEM((64, 1, B), F32),
            pltpu.VMEM((64, 1, B), F32),
            pltpu.VMEM((64, 1, B), F32),
            pltpu.VMEM((256, N), BF16),
            pltpu.VMEM((256, N), BF16),
            pltpu.VMEM((512, 512), BF16),
            pltpu.VMEM((2, 512, 256), BF16),
            pltpu.VMEM((NLEV, B, N), F32),
            pltpu.VMEM((3, 8, B, 16, B), BF16),
            pltpu.VMEM((3, 16, 2, 4, B, B), BF16),
            pltpu.VMEM((4, 2, 16, B, C), BF16),
            pltpu.VMEM((2, 2, 4, B, C), F32),
            pltpu.VMEM((3, 2, 2, 4, B, C), BF16),
            pltpu.VMEM((3, 2, 2, 4, B, C), BF16),
            pltpu.VMEM((4, 2, C, B), F32),
            pltpu.VMEM((4, 2, 2, 4, C, B), BF16),
            pltpu.VMEM((3, 2, 2, 4, 4, H, B), BF16),
            pltpu.VMEM((3, 2, 2, 4, 4, H, B), BF16),
            pltpu.VMEM((3, 2, 2, 4, H, B), BF16),
            pltpu.VMEM((3, 2, 2, 4, H, B), BF16),
            dma, dma, dma, dma, dma((2,)), dma((2,)),
            dma((4,)), dma((3,)), dma((NLEV,)), dma((3, 2)), dma((3, 2, 8)), dma((3, 2)), dma((3, 2)),
            dma((3, 2)), dma((3, 2, 3)), dma((3, 2)), dma((3, 2)), dma((3, 2)), dma((3, 2, 4)), dma((3, 2)), dma((3, 2)),
        ],
        compiler_params=pltpu.CompilerParams(
            collective_id=0, has_side_effects=True, vmem_limit_bytes=50 * 1024 * 1024
        ),
    )(*[pltpu.with_memory_space_constraint(a, pltpu.HBM) for a in (rhs, dest, diag, mask, lower)])


def per_device(rhs_rows, dest_row, diag_inverse, lower_blocks, block_mask):
    dest = dest_row.reshape(1, dest_row.shape[0])
    return solve(rhs_rows, dest, diag_inverse[:, 0], block_mask, lower_blocks)[:, None]


def solution(mesh):
    in_specs = (
        P(("row", "col"), None),
        P(("row", "col")),
        P(None, ("row", "col"), None, None),
        P(None, "row", None, None, "col", None, None),
        P(None, "row", None, "col", None),
    )
    out_specs = P(None, ("row", "col"), None, None)
    return jax.shard_map(per_device, mesh=mesh, in_specs=in_specs, out_specs=out_specs, check_vma=False)
```
